256 devices in a mesh: ctx: 64 (over x, z, core), head: 4 (over y).
Axes of the slice: x: 4, y: 4, z: 8, core: 2. Of those that a mesh axis runs over, the one named last changes fastest.
Arguments:
- queries: bfloat16 [16384, 4096], P('ctx', 'head'), may hold values from -13 to 13
- key_rows: bfloat16 [16384, 4096], P('ctx', 'head'), may hold values from -4 to 4
- value_rows: bfloat16 [16384, 4096], P('ctx', 'head'), may hold values from -14 to 14
- grad_out: bfloat16 [16384, 4096], P('ctx', 'head'), may hold values from -55 to 55
- doc_ids: int32 [16384], P('ctx'), may hold values from 0 to 31, never falling along the last dimension, each value on 1 to 1024 neighbouring positions
- out_gain: float32 [4096], P('head'), may hold values from 0.1 to 1.9
Outputs:
- normed_out: bfloat16 [16384, 4096], P('ctx', 'head')
- grad_query: bfloat16 [16384, 4096], P('ctx', 'head')
- grad_key: bfloat16 [16384, 4096], P('ctx', 'head')
- grad_value: bfloat16 [16384, 4096], P('ctx', 'head')
The draws below stay inside these ranges and needn't reach their ends.
Inputs may be any that keep to these rules, and one draw needn't show every extreme that they name: Along the tokens doc_ids never falls; each of the 32 documents has 1 to 1024 tokens, and one has exactly 1024.
All inputs are finite; a program needn't handle non-finite values.
Results may differ from the reference program's by a relative error of at most 0.0085.
Values sent between devices are 32-bit elements; how exact they have to be, the bound alone decides.
No kernel may reach another device: no remote copies, remote signals or barrier semaphores. Data moves between devices by JAX's collectives and lax.ppermute only.
A program may use at most 192 MiB of HBM per device.

```python
import math
import jax
import jax.numpy as jnp
import numpy as np
from jax import lax

HEADS = 32
HD = 128
TOK_DEV = 256
FEATURES = 4096
TOKENS = 16384
MOST = 1024
DOCS = 32


def rough_field(key, with_rows, with_cols):
    base_key, row_key, col_key = jax.random.split(key, 3)
    frac = jnp.arange(FEATURES, dtype=jnp.float32) / (FEATURES - 1)
    values = jnp.clip(jax.random.normal(base_key, (TOKENS, FEATURES), jnp.float32), -4.0, 4.0)
    row_exp = jax.random.uniform(row_key, (TOKENS, 1), jnp.float32, -0.5, 0.5)
    col_exp = 0.25 * frac - 0.125 + jax.random.uniform(col_key, (FEATURES,), jnp.float32, -0.4, 0.4)
    if with_rows:
        values = values * jnp.power(10.0, row_exp)
    if with_cols:
        values = values * jnp.power(10.0, col_exp)[None, :]
    return values


def draw_queries(key, part):
    return rough_field(jax.random.fold_in(key, 11), True, False).astype(jnp.bfloat16)


def draw_value_rows(key, part):
    return rough_field(jax.random.fold_in(key, 23), False, True).astype(jnp.bfloat16)


def draw_grad_out(key, part):
    return rough_field(jax.random.fold_in(key, 37), True, True).astype(jnp.bfloat16)


def levels(stream_key, extent, cuts, low, top_value):
    factor_of = 1.0
    for axis_at, parts in cuts:
        draws = jax.random.uniform(jax.random.fold_in(jax.random.fold_in(stream_key, 6), axis_at), (parts,), jnp.float32, low / len(cuts), top_value / len(cuts))
        factor_of = factor_of * jnp.repeat(jnp.exp(draws), extent[axis_at] // parts).reshape((-1,) + (1,) * (len(extent) - 1 - axis_at))
    return factor_of


def split_up(number_of, total, bound, slope):
    loads = [(1 << 20) // math.isqrt(grade ** slope) + 1 for grade in range(2, number_of + 1)]
    rest, counts = total - bound - (number_of - 1), [1] * (number_of - 1)
    while rest > 0:
        free = [i for i in range(number_of - 1) if counts[i] < bound]
        pool, remaining = sum([loads[i] for i in free]), rest
        for i in free:
            extra = min(bound - counts[i], max(1, remaining * loads[i] // pool), rest)
            counts[i] = counts[i] + extra
            rest = rest - extra
    return np.array([bound] + counts)


def uneven(own_key, number_of, total, reach, lean):
    if number_of == 2:
        one = jax.random.randint(own_key, (), max(1, total - reach), min(reach, total - 1) + 1)
        return jnp.stack([one, total - one])
    sizes = jnp.asarray(split_up(number_of, total, reach, lean), jnp.int32)
    twos = (number_of - 1) // 2
    giver, receiver = sizes[1:1 + 2 * twos:2], sizes[2:2 + 2 * twos:2]
    margin = jnp.minimum(giver - 1, reach - receiver)
    shifted = jax.random.randint(jax.random.fold_in(own_key, 1), (twos,), 0, 1 << 20) % (margin + 1)
    sizes = sizes.at[1:1 + 2 * twos:2].set(giver - shifted).at[2:2 + 2 * twos:2].set(receiver + shifted)
    return sizes[jax.random.permutation(jax.random.fold_in(own_key, 2), number_of)]


def noise(rng, extent, spread, bound, cuts=(), kind=jnp.bfloat16):
    factor_of = levels(rng, extent, cuts, -0.22, 0.18) if cuts else 1.0
    entries = jax.random.normal(rng, extent, jnp.float32) * spread * factor_of
    return jnp.minimum(jnp.maximum(entries, -bound), bound).astype(kind)


def setup_inputs(seed: int = 0) -> dict:
    splits = jax.random.split(jax.random.key(seed), 7)
    queries = draw_queries(jax.random.fold_in(splits[6], 71), 0)
    key_rows = noise(splits[1], (TOKENS, FEATURES), 1.0, 4.0, ((0, 64), (1, 4)))
    value_rows = draw_value_rows(jax.random.fold_in(splits[6], 71), 0)
    grad_out = draw_grad_out(jax.random.fold_in(splits[6], 71), 0)
    doc_ids = jnp.searchsorted(jnp.cumsum(uneven(splits[4], DOCS, TOKENS, MOST, 2)), jnp.arange(TOKENS), side="right").astype(jnp.int32)
    out_gain = jnp.clip(1.0 + 0.18 * jax.random.normal(splits[5], (FEATURES,), jnp.float32), 0.1, 1.9)
    return dict(queries=queries, key_rows=key_rows, value_rows=value_rows, grad_out=grad_out, doc_ids=doc_ids, out_gain=out_gain)


def visible_mask(docs):
    rows = docs.shape[0]
    position = jnp.arange(rows, dtype=jnp.int32)
    return (docs[:, None] == docs[None, :]) & (position[:, None] >= position[None, :])

def block_scores(q3, k3, docs):
    scores = jnp.einsum('thd,shd->hts', q3.astype(jnp.float32), k3.astype(jnp.float32))
    return jnp.where(visible_mask(docs)[None], scores, 0.0).astype(jnp.bfloat16)

def state_of(args):
    k3, v3, docs = args
    keep = (docs == docs[-1])[:, None, None]
    return jnp.einsum('shd,she->hde', jnp.where(keep, k3, 0).astype(jnp.float32), v3.astype(jnp.float32))

def reference(queries, key_rows, value_rows, grad_out, doc_ids, out_gain):
    blocks = TOKENS // TOK_DEV
    feats = HEADS * HD
    qc = queries.reshape(blocks, TOK_DEV, HEADS, HD)
    kc = key_rows.reshape(blocks, TOK_DEV, HEADS, HD)
    vc = value_rows.reshape(blocks, TOK_DEV, HEADS, HD)
    gc = grad_out.reshape(blocks, TOK_DEV, feats)
    dc = doc_ids.reshape(blocks, TOK_DEV)
    firsts = dc[:, 0]
    lasts = dc[:, -1]
    states = lax.map(state_of, (kc, vc, dc))

    def forward_step(carry, item):
        acc, prev = carry
        state, first, last = item
        carried = jnp.where(prev == first, acc, jnp.zeros_like(acc))
        fresh = jnp.where(last == prev, acc + state, state)
        return ((fresh, last), carried)
    start = (jnp.zeros((HEADS, HD, HD), jnp.float32), jnp.array(-1, jnp.int32))
    _, carried_all = lax.scan(forward_step, start, (states, firsts, lasts))

    def block_forward(args):
        q3, k3, v3, g2, docs, carried = args
        scores = block_scores(q3, k3, docs)
        scores_f = lax.optimization_barrier(scores).astype(jnp.float32)
        carried_b = lax.optimization_barrier(carried.astype(jnp.bfloat16)).astype(jnp.float32)
        in_first = (docs == docs[0])[:, None, None]
        local_part = jnp.einsum('hts,she->the', scores_f, v3.astype(jnp.float32))
        carried_part = jnp.einsum('thd,hde->the', q3.astype(jnp.float32), carried_b)
        attended = (local_part + jnp.where(in_first, carried_part, 0.0)).astype(jnp.bfloat16)
        att32 = attended.reshape(TOK_DEV, feats).astype(jnp.float32)
        weighted = out_gain * g2.astype(jnp.float32)
        inv_rms = lax.rsqrt(lax.optimization_barrier(jnp.sum(att32 * att32, axis=1)) / feats + 1e-06)
        inner = lax.optimization_barrier(jnp.sum(weighted * att32, axis=1)) / feats
        normed = (out_gain * att32 * inv_rms[:, None]).astype(jnp.bfloat16)
        grad_att = (inv_rms[:, None] * weighted - att32 * (inv_rms * inv_rms * inv_rms * inner)[:, None]).astype(jnp.bfloat16)
        grad3 = grad_att.reshape(TOK_DEV, HEADS, HD)
        grad_state = jnp.einsum('thd,the->hde', jnp.where(in_first, q3, 0).astype(jnp.float32), grad3.astype(jnp.float32))
        return (normed, grad3, grad_state)
    normed_all, grad_all, grad_states = lax.map(block_forward, (qc, kc, vc, gc, dc, carried_all))

    def backward_step(carry, item):
        acc, nxt = carry
        state, first, last = item
        later = jnp.where(nxt == last, acc, jnp.zeros_like(acc))
        fresh = jnp.where(first == nxt, acc + state, state)
        return ((fresh, first), later)
    _, later_all = lax.scan(backward_step, start, (grad_states, firsts, lasts), reverse=True)

    def block_backward(args):
        q3, k3, v3, g3, docs, carried, later = args
        scores_f = lax.optimization_barrier(block_scores(q3, k3, docs)).astype(jnp.float32)
        q32 = q3.astype(jnp.float32)
        k32 = k3.astype(jnp.float32)
        v32 = v3.astype(jnp.float32)
        g32 = g3.astype(jnp.float32)
        grad_sc = jnp.einsum('the,she->hts', g32, v32)
        grad_sc = jnp.where(visible_mask(docs)[None], grad_sc, 0.0).astype(jnp.bfloat16)
        grad_sc = lax.optimization_barrier(grad_sc).astype(jnp.float32)
        carried_b = lax.optimization_barrier(carried.astype(jnp.bfloat16)).astype(jnp.float32)
        later_b = lax.optimization_barrier(later.astype(jnp.bfloat16)).astype(jnp.float32)
        in_first = (docs == docs[0])[:, None, None]
        in_last = (docs == docs[-1])[:, None, None]
        grad_q = jnp.einsum('hts,shd->thd', grad_sc, k32) + jnp.where(in_first, jnp.einsum('the,hde->thd', g32, carried_b), 0.0)
        grad_k = jnp.einsum('hts,thd->shd', grad_sc, q32) + jnp.where(in_last, jnp.einsum('she,hde->shd', v32, later_b), 0.0)
        grad_v = jnp.einsum('hts,the->she', scores_f, g32) + jnp.where(in_last, jnp.einsum('shd,hde->she', k32, later_b), 0.0)
        return (grad_q.astype(jnp.bfloat16), grad_k.astype(jnp.bfloat16), grad_v.astype(jnp.bfloat16))
    grad_q, grad_k, grad_v = lax.map(block_backward, (qc, kc, vc, grad_all, dc, carried_all, later_all))
    return (normed_all.reshape(TOKENS, feats), grad_q.reshape(TOKENS, feats), grad_k.reshape(TOKENS, feats), grad_v.reshape(TOKENS, feats))
```

```python
import jax
import jax.numpy as jnp
from jax import lax
from jax.experimental import pallas as pl
from jax.experimental.pallas import tpu as pltpu
from jax.sharding import PartitionSpec as P

HEADS = 32
HD = 128
TAG = 8
F32 = jnp.float32
BF16 = jnp.bfloat16


def dot(a, b, dims):
    return lax.dot_general(a, b, (dims, ((), ())), preferred_element_type=F32)


NN = ((1,), (0,))
NT = ((1,), (1,))
TN = ((0,), (0,))


def as_column(row):
    return jnp.transpose(jnp.broadcast_to(row, (HD, row.shape[1])))


def head(h):
    return slice(h * HD, (h + 1) * HD)


def in_doc(row_ref, which):
    return (as_column(row_ref[...].astype(F32)) == which.astype(F32)).astype(F32)


def visible(row_ref):
    rows = row_ref.shape[1]
    row = row_ref[...].astype(F32)
    column = as_column(row)
    column = jnp.concatenate([column] * (rows // HD), axis=1)
    t = lax.broadcasted_iota(jnp.int32, (rows, rows), 0)
    s = lax.broadcasted_iota(jnp.int32, (rows, rows), 1)
    return (column == jnp.broadcast_to(row, (rows, rows))) & (t >= s)


def state_kernel(ids, row, k, v, out):
    rows = k.shape[0]
    last = ids[rows - 1]
    keep = in_doc(row, last).astype(BF16)
    for h in range(k.shape[1] // HD):
        out[head(h), :] = dot(k[:, head(h)] * keep, v[:, head(h)], TN)
    out[k.shape[1]:, :] = jnp.full((TAG, HD), last.astype(F32))


def local_kernel(row, q, k, v, after, scores, part):
    del after
    seen = visible(row)
    for h in range(q.shape[1] // HD):
        sc = dot(q[:, head(h)], k[:, head(h)], NT)
        sc = jnp.where(seen, sc, 0.0).astype(BF16)
        scores[h] = sc
        part[:, head(h)] = dot(sc, v[:, head(h)], NN)


def attend_kernel(ids, row, q, part, came, grad, gain, attended, carried, stats):
    rows, width = q.shape
    first = ids[0]
    keep = in_doc(row, first)
    same = came[width:width + 1, :] == first.astype(F32)
    square = jnp.zeros((rows, HD), F32)
    inner = jnp.zeros((rows, HD), F32)
    for h in range(width // HD):
        state = jnp.where(same, came[head(h), :], 0.0).astype(BF16)
        carried[head(h), :] = state
        att = (part[:, head(h)] + keep * dot(q[:, head(h)], state, NN)).astype(BF16)
        attended[:, head(h)] = att
        att = att.astype(F32)
        square = square + att * att
        inner = inner + gain[:, head(h)] * grad[:, head(h)].astype(F32) * att
    ones = jnp.ones((TAG, HD), F32)
    upper = lax.broadcasted_iota(jnp.int32, (TAG, rows), 0) < TAG // 2
    exact = lax.Precision.HIGHEST
    sums = [
        lax.dot_general(ones, x, (NT, ((), ())), precision=exact, preferred_element_type=F32)
        for x in (square, inner)
    ]
    stats[...] = jnp.where(upper, sums[0], sums[1])


def norm_scales(stats):
    feats = HEADS * HD
    inv = lax.rsqrt(stats[0:1, :] / feats + 1e-06)
    back = inv * inv * inv * (stats[TAG - 1:TAG, :] / feats)
    return as_column(inv), as_column(back)


def grad_kernel(ids, row, q, attended, grad, gain, stats, g_out, out):
    rows, width = q.shape
    first = ids[0]
    keep = in_doc(row, first).astype(BF16)
    inv, back = norm_scales(stats[...])
    for h in range(width // HD):
        weighted = gain[:, head(h)] * grad[:, head(h)].astype(F32)
        g = (inv * weighted - attended[:, head(h)].astype(F32) * back).astype(BF16)
        g_out[:, head(h)] = g
        out[head(h), :] = dot(q[:, head(h)] * keep, g, TN)
    out[width:, :] = jnp.full((TAG, HD), first.astype(F32))


def back_kernel(ids, row, q, k, v, g, scores, attended, carried, gain, stats, after,
                normed, grad_q, part_k, part_v):
    del after
    rows, width = q.shape
    keep = in_doc(row, ids[0])
    seen = visible(row)
    inv, _ = norm_scales(stats[...])
    for h in range(width // HD):
        gh = g[:, head(h)]
        normed[:, head(h)] = (gain[:, head(h)] * attended[:, head(h)].astype(F32) * inv).astype(BF16)
        gs = dot(gh, v[:, head(h)], NT)
        gs = jnp.where(seen, gs, 0.0).astype(BF16)
        whole = dot(gs, k[:, head(h)], NN) + keep * dot(gh, carried[head(h), :], NT)
        grad_q[:, head(h)] = whole.astype(BF16)
        part_k[:, head(h)] = dot(gs, q[:, head(h)], TN)
        part_v[:, head(h)] = dot(scores[h], gh, TN)


def last_kernel(ids, row, k, v, part_k, part_v, came, grad_k, grad_v):
    rows, width = k.shape
    last = ids[rows - 1]
    keep = in_doc(row, last)
    same = came[width:width + 1, :] == last.astype(F32)
    for h in range(width // HD):
        later = jnp.where(same, came[head(h), :], 0.0).astype(BF16)
        grad_k[:, head(h)] = (part_k[:, head(h)] + keep * dot(v[:, head(h)], later, NT)).astype(BF16)
        grad_v[:, head(h)] = (part_v[:, head(h)] + keep * dot(k[:, head(h)], later, NN)).astype(BF16)


def call(kernel, outs, *args, smem=0):
    specs = [pl.BlockSpec(memory_space=pltpu.SMEM)] * smem
    specs += [pl.BlockSpec(memory_space=pltpu.VMEM)] * (len(args) - smem)
    out_specs = [pl.BlockSpec(memory_space=pltpu.VMEM)] * len(outs)
    return pl.pallas_call(
        kernel,
        out_shape=[jax.ShapeDtypeStruct(shape, kind) for shape, kind in outs],
        in_specs=specs,
        out_specs=out_specs,
        compiler_params=pltpu.CompilerParams(vmem_limit_bytes=40 * 1024 * 1024),
        name=kernel.__name__,
    )(*args)


def joined(mine, came):
    width = mine.shape[0] - TAG
    same = mine[width, 0] == came[width, 0]
    inside = lax.broadcasted_iota(jnp.int32, mine.shape, 0) < width
    return mine + jnp.where(same & inside, came, 0.0)


def carry(states, blocks, backward):
    chips = blocks // 2

    def hop(value, source, target, apart):
        pairs = [
            (2 * c + source, 2 * (c + apart) + target) for c in range(chips) if c + apart < chips
        ]
        if backward:
            pairs = [(blocks - 1 - a, blocks - 1 - b) for a, b in pairs]
        return lax.ppermute(value, "ctx", pairs)

    both = joined(states, hop(states, 0, 1, 0))
    window = joined(both, hop(both, 1, 1, 1))
    entering = hop(window, 1, 0, 1)
    passed = hop(joined(states, entering), 0, 1, 0)
    return entering + passed, both


def local(queries, key_rows, value_rows, grad_out, doc_ids, out_gain):
    rows, width = queries.shape
    heads = width // HD
    blocks = lax.axis_size("ctx")
    ranks = lax.axis_size("head")
    row = doc_ids.reshape(1, rows)
    gain = out_gain.reshape(1, width)
    wide, half, state = ((rows, width), F32), ((rows, width), BF16), ((width + TAG, HD), F32)

    (states,) = call(state_kernel, [state], doc_ids, row, key_rows, value_rows, smem=1)
    came, both = carry(states, blocks, False)
    scores, part = call(
        local_kernel, [((heads, rows, rows), BF16), wide],
        row, queries, key_rows, value_rows, both[width:],
    )
    attended, carried, stats = call(
        attend_kernel, [half, ((width, HD), BF16), ((TAG, rows), F32)],
        doc_ids, row, queries, part, came, grad_out, gain, smem=1,
    )
    total = stats
    for apart in range(1, ranks):
        total = total + lax.ppermute(
            stats, "head", [(i, (i + apart) % ranks) for i in range(ranks)]
        )
    g, grads = call(
        grad_kernel, [half, state],
        doc_ids, row, queries, attended, grad_out, gain, total, smem=1,
    )
    came, both = carry(grads, blocks, True)
    normed, grad_q, part_k, part_v = call(
        back_kernel, [half, half, wide, wide],
        doc_ids, row, queries, key_rows, value_rows, g, scores, attended, carried, gain, total,
        both[width:], smem=1,
    )
    grad_k, grad_v = call(
        last_kernel, [half, half],
        doc_ids, row, key_rows, value_rows, part_k, part_v, came, smem=1,
    )
    return normed, grad_q, grad_k, grad_v


def solution(mesh):
    cut = P("ctx", "head")
    return jax.shard_map(
        local,
        mesh=mesh,
        in_specs=(cut, cut, cut, cut, P("ctx"), P("head")),
        out_specs=(cut, cut, cut, cut),
        check_vma=False,
    )
```

```python
import jax
import jax.numpy as jnp
from jax import lax
from jax.experimental import pallas as pl
from jax.experimental.pallas import tpu as pltpu
from jax.sharding import PartitionSpec as P

HEADS = 32
HD = 128
TAG = 8
F32 = jnp.float32
BF16 = jnp.bfloat16


def dot(a, b, dims):
    return lax.dot_general(a, b, (dims, ((), ())), preferred_element_type=F32)


NN = ((1,), (0,))
NT = ((1,), (1,))
TN = ((0,), (0,))


def as_column(row):
    return jnp.transpose(jnp.broadcast_to(row, (HD, row.shape[1])))


def head(h):
    return slice(h * HD, (h + 1) * HD)


def in_doc(row_ref, at):
    row = row_ref[...].astype(F32)
    which = jnp.broadcast_to(row[:, at:at + 1], (row.shape[1], HD))
    return (as_column(row) == which).astype(F32)


def tag(row_ref, at):
    return jnp.broadcast_to(row_ref[:, at:at + 1].astype(F32), (1, HD))


def visible(row_ref):
    rows = row_ref.shape[1]
    row = row_ref[...].astype(F32)
    column = as_column(row)
    column = jnp.concatenate([column] * (rows // HD), axis=1)
    t = lax.broadcasted_iota(jnp.int32, (rows, rows), 0)
    s = lax.broadcasted_iota(jnp.int32, (rows, rows), 1)
    return (column == jnp.broadcast_to(row, (rows, rows))) & (t >= s)


def state_kernel(lo, hi, row_hbm, k_hbm, v_hbm, out, row, k, v, sems):
    rows = k.shape[0]
    width = (hi - lo) * HD
    span = slice(lo * HD, hi * HD)
    copies = [
        pltpu.make_async_copy(row_hbm, row, sems.at[0]),
        pltpu.make_async_copy(k_hbm.at[:, span], k, sems.at[1]),
        pltpu.make_async_copy(v_hbm.at[:, span], v, sems.at[2]),
    ]
    for copy in copies:
        copy.start()
    copies[0].wait()
    keep = in_doc(row, rows - 1).astype(BF16)
    out[width:, :] = jnp.broadcast_to(tag(row, rows - 1), (TAG, HD))
    copies[1].wait()
    copies[2].wait()
    for h in range(hi - lo):
        out[head(h), :] = dot(k[:, head(h)] * keep, v[:, head(h)], TN)


def merge_kernel(mine, came, *rest):
    out = rest[-1]
    width = mine.shape[0] - TAG
    same = mine[width:width + 1, :] == came[width:width + 1, :]
    out[:width, :] = mine[:width, :] + jnp.where(same, came[:width, :], 0.0)
    out[width:, :] = mine[width:, :]


def local_kernel(row, q, k, v, after, scores, part):
    del after
    seen = visible(row)
    for h in range(q.shape[1] // HD):
        sc = dot(q[:, head(h)], k[:, head(h)], NT)
        sc = jnp.where(seen, sc, 0.0).astype(BF16)
        scores[h] = sc
        part[:, head(h)] = dot(sc, v[:, head(h)], NN)


def attend_kernel(lo, hi, row, q, part, entering, passed, grad, gain, *rest):
    attended, carried, stats = rest[-3:]
    rows = q.shape[0]
    width = (hi - lo) * HD
    keep = in_doc(row, 0)
    came = entering[width:width + 1, :] + passed[width:width + 1, :]
    same = came == tag(row, 0)
    square = jnp.zeros((rows, HD), F32)
    inner = jnp.zeros((rows, HD), F32)
    for h in range(hi - lo):
        at = head(lo + h)
        state = jnp.where(same, entering[head(h), :] + passed[head(h), :], 0.0).astype(BF16)
        carried[head(h), :] = state
        att = (part[:, at] + keep * dot(q[:, at], state, NN)).astype(BF16)
        attended[:, head(h)] = att
        att = att.astype(F32)
        square = square + att * att
        inner = inner + gain[:, at] * grad[:, at].astype(F32) * att
    ones = jnp.ones((TAG, HD), F32)
    upper = lax.broadcasted_iota(jnp.int32, (TAG, rows), 0) < TAG // 2
    exact = lax.Precision.HIGHEST
    sums = [
        lax.dot_general(ones, x, (NT, ((), ())), precision=exact, preferred_element_type=F32)
        for x in (square, inner)
    ]
    sums = jnp.where(upper, sums[0], sums[1])
    stats[...] = sums + rest[0][...] if len(rest) > 3 else sums


def norm_scales(parts):
    feats = HEADS * HD
    total = parts[0][...]
    for x in parts[1:]:
        total = total + x[...]
    inv = lax.rsqrt(total[0:1, :] / feats + 1e-06)
    back = inv * inv * inv * (total[TAG - 1:TAG, :] / feats)
    return as_column(inv), as_column(back)


def grad_kernel(lo, hi, ranks, row, q, attended, grad, gain, *rest):
    g_out, out = rest[-2:]
    rows = q.shape[0]
    width = (hi - lo) * HD
    keep = in_doc(row, 0).astype(BF16)
    inv, back = norm_scales(rest[:ranks])
    for h in range(hi - lo):
        at = head(lo + h)
        weighted = gain[:, at] * grad[:, at].astype(F32)
        g = (inv * weighted - attended[:, head(h)].astype(F32) * back).astype(BF16)
        g_out[:, head(h)] = g
        out[head(h), :] = dot(q[:, at] * keep, g, TN)
    out[width:, :] = jnp.broadcast_to(tag(row, 0), (TAG, HD))


def back_kernel(cuts, ranks, row, q, k, v, scores, gain, *rest):
    normed, grad_q, part_k, part_v = rest[-4:]
    n = len(cuts)
    inv, _ = norm_scales(rest[3 * n:3 * n + ranks])
    keep = in_doc(row, 0)
    seen = visible(row)
    for c, (lo, hi) in enumerate(cuts):
        g, attended, carried = rest[c], rest[n + c], rest[2 * n + c]
        for h in range(hi - lo):
            at = head(lo + h)
            gh = g[:, head(h)]
            att = attended[:, head(h)].astype(F32)
            normed[:, at] = (gain[:, at] * att * inv).astype(BF16)
            gs = dot(gh, v[:, at], NT)
            gs = jnp.where(seen, gs, 0.0).astype(BF16)
            whole = dot(gs, k[:, at], NN) + keep * dot(gh, carried[head(h), :], NT)
            grad_q[:, at] = whole.astype(BF16)
            part_k[:, at] = dot(gs, q[:, at], TN)
            part_v[:, at] = dot(scores[lo + h], gh, TN)


def last_kernel(lo, hi, row, k, v, part_k, part_v, entering, passed, *rest):
    k_hbm, v_hbm, grad_k, grad_v, sems = rest[-5:]
    rows = k.shape[0]
    width = (hi - lo) * HD
    keep = in_doc(row, rows - 1)
    came = entering[width:width + 1, :] + passed[width:width + 1, :]
    same = came == tag(row, rows - 1)
    copies = []
    for h in range(hi - lo):
        at = head(lo + h)
        later = jnp.where(same, entering[head(h), :] + passed[head(h), :], 0.0).astype(BF16)
        grad_k[:, head(h)] = (part_k[:, at] + keep * dot(v[:, at], later, NT)).astype(BF16)
        grad_v[:, head(h)] = (part_v[:, at] + keep * dot(k[:, at], later, NN)).astype(BF16)
        for i, (held, out) in enumerate(((grad_k, k_hbm), (grad_v, v_hbm))):
            copies.append(pltpu.make_async_copy(held.at[:, head(h)], out.at[:, at], sems.at[2 * h + i]))
            copies[-1].start()
    for copy in copies:
        copy.wait()


VMEM, HBM, ANY = pltpu.VMEM, pltpu.HBM, pl.ANY


def call(kernel, name, outs, args, spaces=(), after=(), out_space=VMEM, scratch=(), aliases={}):
    spaces = list(spaces) + [VMEM] * (len(args) - len(spaces)) + [ANY] * len(after)
    return pl.pallas_call(
        kernel,
        out_shape=[jax.ShapeDtypeStruct(shape, kind) for shape, kind in outs],
        in_specs=[pl.BlockSpec(memory_space=space) for space in spaces],
        out_specs=[pl.BlockSpec(memory_space=out_space)] * len(outs),
        scratch_shapes=scratch,
        input_output_aliases=aliases,
        compiler_params=pltpu.CompilerParams(vmem_limit_bytes=40 * 1024 * 1024),
        name=name,
    )(*args, *after)


def merge(mine, came, after=()):
    return call(merge_kernel, "merge", [(mine.shape, F32)], [mine, came], after=after)[0]


def carry(states, blocks, backward, beside):
    chips = blocks // 2

    def hop(value, source, target, apart):
        pairs = [
            (2 * c + source, 2 * (c + apart) + target) for c in range(chips) if c + apart < chips
        ]
        if backward:
            pairs = [(blocks - 1 - a, blocks - 1 - b) for a, b in pairs]
        return lax.ppermute(value, "ctx", pairs)

    both = [merge(s, hop(s, 0, 1, 0)) for s in states]
    once = [hop(b, 1, 1, 1) for b in both]
    work, token = beside(both[-1])
    window = [merge(b, o, [token]) for b, o in zip(both, once)]
    entering = [hop(w, 1, 0, 1) for w in window]
    passed = [hop(merge(s, e), 0, 1, 0) for s, e in zip(states, entering)]
    return list(zip(entering, passed)), work


CUTS = ((0, 4), (4, 8))


def local(queries, key_rows, value_rows, grad_out, doc_ids, out_gain):
    rows, width = queries.shape
    heads = width // HD
    blocks = lax.axis_size("ctx")
    ranks = lax.axis_size("head")
    row = doc_ids.reshape(1, rows)
    gain = out_gain.reshape(1, width)
    wide, half, sums = ((rows, width), F32), ((rows, width), BF16), ((TAG, rows), F32)

    def of(cut, *rest):
        return ((cut[1] - cut[0]) * HD, *rest)

    def bind(kernel, *fixed):
        return lambda *refs: kernel(*fixed, *refs)

    states = [
        call(
            bind(state_kernel, *cut), "state", [((of(cut)[0] + TAG, HD), F32)],
            [pltpu.with_memory_space_constraint(x, HBM) for x in (row, key_rows, value_rows)],
            spaces=[HBM] * 3,
            scratch=[VMEM((1, rows), jnp.int32), VMEM((rows, *of(cut)), BF16),
                     VMEM((rows, *of(cut)), BF16), pltpu.SemaphoreType.DMA((3,))],
        )[0]
        for cut in CUTS
    ]

    def local_work(held):
        scores, part = call(
            local_kernel, "local", [((heads, rows, rows), BF16), wide],
            [row, queries, key_rows, value_rows], after=[held],
        )
        return (scores, part), part

    came, (scores, part) = carry(states, blocks, False, local_work)
    attended, carried, stats = [], [], []
    for cut, pair in zip(CUTS, came):
        out = call(
            bind(attend_kernel, *cut), "attend",
            [((rows, *of(cut)), BF16), (of(cut, HD), BF16), sums],
            [row, queries, part, *pair, grad_out, gain, *stats[-1:]],
        )
        for held, new in zip((attended, carried, stats), out):
            held.append(new)
    stats = stats[-1:]
    stats += [
        lax.ppermute(stats[0], "head", [(i, (i + apart) % ranks) for i in range(ranks)])
        for apart in range(1, ranks)
    ]
    g, grads = [], []
    for cut, att in zip(CUTS, attended):
        out = call(
            bind(grad_kernel, *cut, ranks), "grad",
            [((rows, *of(cut)), BF16), ((of(cut)[0] + TAG, HD), F32)],
            [row, queries, att, grad_out, gain, *stats],
        )
        g.append(out[0])
        grads.append(out[1])

    def back_work(held):
        out = call(
            bind(back_kernel, CUTS, ranks), "back", [half, half, wide, wide],
            [row, queries, key_rows, value_rows, scores, gain, *g, *attended, *carried, *stats],
            after=[held],
        )
        return out, out[2]

    came, (normed, grad_q, part_k, part_v) = carry(grads, blocks, True, back_work)
    done = ()
    for cut, pair in zip(CUTS, came):
        n = 7
        done = call(
            bind(last_kernel, *cut), "last", [half, half],
            [row, key_rows, value_rows, part_k, part_v, *pair], after=done, out_space=HBM,
            scratch=[VMEM((rows, *of(cut)), BF16), VMEM((rows, *of(cut)), BF16),
                     pltpu.SemaphoreType.DMA((2 * (cut[1] - cut[0]),))],
            aliases={n: 0, n + 1: 1} if done else {},
        )
    return normed, grad_q, *done


def solution(mesh):
    cut = P("ctx", "head")
    return jax.shard_map(
        local,
        mesh=mesh,
        in_specs=(cut, cut, cut, cut, P("ctx"), P("head")),
        out_specs=(cut, cut, cut, cut),
        check_vma=False,
    )
```

```python
import jax
import jax.numpy as jnp
from jax import lax
from jax.experimental import pallas as pl
from jax.experimental.pallas import tpu as pltpu
from jax.sharding import PartitionSpec as P

HEADS = 32
HD = 128
TAG = 8
F32 = jnp.float32
BF16 = jnp.bfloat16
VMEM, HBM, ANY = pltpu.VMEM, pltpu.HBM, pl.ANY
DMA = pltpu.SemaphoreType.DMA
NN = ((1,), (0,))
NT = ((1,), (1,))
TN = ((0,), (0,))


def dot(a, b, dims):
    return lax.dot_general(a, b, (dims, ((), ())), preferred_element_type=F32)


def head(h):
    return slice(h * HD, (h + 1) * HD)


def core():
    return lax.rem(lax.axis_index("ctx"), 2)


def columns(half, width):
    at = core() if half == 0 else 1 - core()
    return pl.ds(pl.multiple_of(at * width, width), width)


def as_column(row):
    return jnp.transpose(jnp.broadcast_to(row, (HD, row.shape[1])))


def in_doc(row_ref, at):
    row = row_ref[...].astype(F32)
    which = jnp.broadcast_to(row[:, at:at + 1], (row.shape[1], HD))
    return (as_column(row) == which).astype(F32)


def tag(row_ref, at):
    return jnp.broadcast_to(row_ref[:, at:at + 1].astype(F32), (1, HD))


def visible(row_ref):
    rows = row_ref.shape[1]
    row = row_ref[...].astype(F32)
    column = as_column(row)
    column = jnp.concatenate([column] * (rows // HD), axis=1)
    t = lax.broadcasted_iota(jnp.int32, (rows, rows), 0)
    s = lax.broadcasted_iota(jnp.int32, (rows, rows), 1)
    return (column == jnp.broadcast_to(row, (rows, rows))) & (t >= s)


def state_kernel(half, row_hbm, k_hbm, v_hbm, *rest):
    out, k, v, row, sems = rest[-5:]
    rows, width = k.shape
    span = columns(half, width)
    copies = [
        pltpu.make_async_copy(row_hbm, row, sems.at[0]),
        pltpu.make_async_copy(k_hbm.at[:, span], k, sems.at[1]),
        pltpu.make_async_copy(v_hbm.at[:, span], v, sems.at[2]),
    ]
    for copy in copies:
        copy.start()
    copies[0].wait()
    keep = in_doc(row, rows - 1).astype(BF16)
    out[width:, :] = jnp.broadcast_to(tag(row, rows - 1), (TAG, HD))
    copies[1].wait()
    copies[2].wait()
    for h in range(width // HD):
        out[head(h), :] = dot(k[:, head(h)] * keep, v[:, head(h)], TN)


def add_into(out, near, far, near_lo, far_lo):
    size = out.shape[0] - TAG
    near_tag = near[near.shape[0] - TAG:, :]
    same = near_tag[0:1, :] == far[far.shape[0] - TAG:far.shape[0] - TAG + 1, :]
    here = far[far_lo:far_lo + size, :]
    out[:size, :] = near[near_lo:near_lo + size, :] + jnp.where(same, here, 0.0)
    out[size:, :] = near_tag


def pair_kernel(backward, mine, came, *outs):
    size = outs[0].shape[0] - TAG
    upstream = core() == int(backward)

    def fill(down, up):
        for i, out in enumerate(outs):
            add_into(out, down, up, i * size, i * size)

    pl.when(upstream)(lambda: fill(came, mine))
    pl.when(jnp.logical_not(upstream))(lambda: fill(mine, came))


def merge_kernel(near, far, *rest):
    add_into(rest[-1], near, far, 0, 0)


def split_kernel(backward, part, entering, mine, came, keep, send):
    size = entering.shape[0] - TAG
    upstream = core() == int(backward)

    def fill(to_up, to_down, up):
        to_up[...] = entering[...]
        add_into(to_down, up, entering, part * size, 0)

    pl.when(upstream)(lambda: fill(keep, send, mine))
    pl.when(jnp.logical_not(upstream))(lambda: fill(send, keep, came))


def local_kernel(row, k0, k1, v0, v1, q_hbm, grad_hbm, gain_hbm, *rest):
    scores, part, q, weighted, gain, grad, sems = rest[-7:]
    rows, width = k0.shape
    copies = []
    for i, (hbm, held) in enumerate(((q_hbm, q), (gain_hbm, gain), (grad_hbm, grad))):
        for half in range(2):
            at = slice(half * width, (half + 1) * width)
            copies.append(
                pltpu.make_async_copy(
                    hbm.at[:, columns(half, width)], held.at[:, at], sems.at[2 * i + half]
                )
            )
            copies[-1].start()
    seen = visible(row)
    copies[0].wait()
    copies[1].wait()
    n = width // HD
    for h in range(2 * n):
        k, v = (k0, v0) if h < n else (k1, v1)
        sc = dot(q[:, head(h)], k[:, head(h % n)], NT)
        sc = jnp.where(seen, sc, 0.0).astype(BF16)
        scores[h] = sc
        part[:, head(h)] = dot(sc, v[:, head(h % n)], NN)
    for copy in copies[2:]:
        copy.wait()
    for h in range(2 * n):
        weighted[:, head(h)] = gain[:, head(h)] * grad[:, head(h)].astype(F32)


def pieces(refs):
    for ref in refs:
        size = ref.shape[0] - TAG
        for h in range(size // HD):
            yield ref[head(h), :], ref[size:size + 1, :]


def attend_kernel(half, chunks, row, q, part, weighted, *rest):
    came, rest = rest[:chunks], rest[chunks:]
    attended, carried, stats = rest[-3:]
    rows, width = attended.shape
    keep = in_doc(row, 0)
    first = tag(row, 0)
    square = jnp.zeros((rows, HD), F32)
    inner = jnp.zeros((rows, HD), F32)
    for h, (state, its) in enumerate(pieces(came)):
        at = head(half * (width // HD) + h)
        state = jnp.where(its == first, state, 0.0).astype(BF16)
        carried[head(h), :] = state
        att = (part[:, at] + keep * dot(q[:, at], state, NN)).astype(BF16)
        attended[:, head(h)] = att
        att = att.astype(F32)
        square = square + att * att
        inner = inner + weighted[:, at] * att
    ones = jnp.ones((TAG, HD), F32)
    upper = lax.broadcasted_iota(jnp.int32, (TAG, rows), 0) < TAG // 2
    exact = lax.Precision.HIGHEST
    sums = [
        lax.dot_general(ones, x, (NT, ((), ())), precision=exact, preferred_element_type=F32)
        for x in (square, inner)
    ]
    sums = jnp.where(upper, sums[0], sums[1])
    stats[...] = sums + rest[0][...] if len(rest) > 3 else sums


def norm_scales(parts):
    feats = HEADS * HD
    total = parts[0][...]
    for x in parts[1:]:
        total = total + x[...]
    inv = lax.rsqrt(total[0:1, :] / feats + 1e-06)
    back = inv * inv * inv * (total[TAG - 1:TAG, :] / feats)
    return as_column(inv), as_column(back)


def grad_kernel(half, ranks, row, q, weighted, attended, *rest):
    g_out, out = rest[-2:]
    rows, width = attended.shape
    keep = in_doc(row, 0).astype(BF16)
    inv, back = norm_scales(rest[:ranks])
    for h in range(width // HD):
        at = head(half * (width // HD) + h)
        g = (inv * weighted[:, at] - attended[:, head(h)].astype(F32) * back).astype(BF16)
        g_out[:, head(h)] = g
        out[head(h), :] = dot(q[:, at] * keep, g, TN)
    out[width:, :] = jnp.broadcast_to(tag(row, 0), (TAG, HD))


def back_kernel(ranks, row, q, scores, gain, k0, k1, v0, v1, g0, g1, a0, a1, c0, c1, *rest):
    normed_hbm, grad_q_hbm, part_k, part_v, normed, grad_q, sems = rest[-7:]
    rows, width = k0.shape
    inv, _ = norm_scales(rest[:ranks])
    keep = in_doc(row, 0)
    seen = visible(row)
    n = width // HD
    copies = []
    for half, (k, v, g, attended, carried) in enumerate(((k0, v0, g0, a0, c0), (k1, v1, g1, a1, c1))):
        for h in range(n):
            at = head(half * n + h)
            gh = g[:, head(h)]
            normed[:, at] = (gain[:, at] * attended[:, head(h)].astype(F32) * inv).astype(BF16)
            gs = dot(gh, v[:, head(h)], NT)
            gs = jnp.where(seen, gs, 0.0).astype(BF16)
            whole = dot(gs, k[:, head(h)], NN) + keep * dot(gh, carried[head(h), :], NT)
            grad_q[:, at] = whole.astype(BF16)
            part_k[:, at] = dot(gs, q[:, at], TN)
            part_v[:, at] = dot(scores[half * n + h], gh, TN)
        span = slice(half * width, (half + 1) * width)
        for i, (held, out) in enumerate(((normed, normed_hbm), (grad_q, grad_q_hbm))):
            copies.append(
                pltpu.make_async_copy(
                    held.at[:, span], out.at[:, columns(half, width)], sems.at[2 * half + i]
                )
            )
            copies[-1].start()
    for copy in copies:
        copy.wait()


def last_kernel(half, chunks, row, k, v, part_k, part_v, *rest):
    came = rest[:chunks]
    k_hbm, v_hbm, grad_k, grad_v, sems = rest[-5:]
    rows, width = k.shape
    keep = in_doc(row, rows - 1)
    last = tag(row, rows - 1)
    at_core = core() if half == 0 else 1 - core()
    copies = []
    for h, (state, its) in enumerate(pieces(came)):
        at = head(half * (width // HD) + h)
        later = jnp.where(its == last, state, 0.0).astype(BF16)
        grad_k[:, head(h)] = (part_k[:, at] + keep * dot(v[:, head(h)], later, NT)).astype(BF16)
        grad_v[:, head(h)] = (part_v[:, at] + keep * dot(k[:, head(h)], later, NN)).astype(BF16)
        span = pl.ds(pl.multiple_of(at_core * width + h * HD, HD), HD)
        for i, (held, out) in enumerate(((grad_k, k_hbm), (grad_v, v_hbm))):
            copies.append(
                pltpu.make_async_copy(held.at[:, head(h)], out.at[:, span], sems.at[2 * h + i])
            )
            copies[-1].start()
    for copy in copies:
        copy.wait()


def call(kernel, fixed, outs, args, after=(), scratch=(), aliases={}):
    spaces = [HBM if isinstance(x, list) else VMEM for x in args] + [ANY] * len(after)
    args = [
        pltpu.with_memory_space_constraint(x[0], HBM) if isinstance(x, list) else x for x in args
    ]
    return pl.pallas_call(
        lambda *refs: kernel(*fixed, *refs),
        out_shape=[jax.ShapeDtypeStruct(*out[:2]) for out in outs],
        in_specs=[pl.BlockSpec(memory_space=space) for space in spaces],
        out_specs=[pl.BlockSpec(memory_space=(*out, VMEM)[2]) for out in outs],
        scratch_shapes=scratch,
        input_output_aliases=aliases,
        compiler_params=pltpu.CompilerParams(vmem_limit_bytes=40 * 1024 * 1024),
        name=kernel.__name__[:-7],
    )(*args, *after)


def carry(mine, other, chunks, backward, beside):
    blocks = lax.axis_size("ctx")
    step = -2 if backward else 2

    def swap(value):
        return lax.ppermute(value, "ctx", [(i, i ^ 1) for i in range(blocks)])

    def hop(value):
        return lax.ppermute(value, "ctx", [(i, (i + step) % blocks) for i in range(blocks)])

    sent = other()
    came = swap(sent)
    mine = mine(sent)
    size = (mine.shape[0] - TAG) // chunks
    chunk = ((size + TAG, HD), F32)
    both = call(pair_kernel, [backward], [chunk] * chunks, [mine, came])
    once = [hop(b) for b in both]
    work, token = beside(both[-1])
    window = [call(merge_kernel, [], [chunk], [b, o], [token])[0] for b, o in zip(both, once)]
    entering = [hop(w) for w in window]
    keep, back = [], []
    for i, e in enumerate(entering):
        kept, send = call(split_kernel, [backward, i], [chunk] * 2, [e, mine, came])
        keep.append(kept)
        back.append(swap(send))
    return keep, back, work


CHUNKS = 2


def local(queries, key_rows, value_rows, grad_out, doc_ids, out_gain):
    rows, width = queries.shape
    heads = width // HD
    part_width = width // 2
    ranks = lax.axis_size("head")
    row = doc_ids.reshape(1, rows)
    gain = out_gain.reshape(1, width)
    wide, half, sums = ((rows, width), F32), ((rows, part_width), BF16), ((TAG, rows), F32)
    state = ((part_width + TAG, HD), F32)

    held = {}

    def make_state(which, after=()):
        out, held["k", which], held["v", which] = call(
            state_kernel, [which], [state, half, half], [[row], [key_rows], [value_rows]],
            after=after, scratch=[VMEM((1, rows), jnp.int32), DMA((3,))],
        )
        return out

    def local_work(token):
        out = call(
            local_kernel, [],
            [((heads, rows, rows), BF16), wide, ((rows, width), BF16), wide, ((1, width), F32)],
            [row, *k, *v, [queries], [grad_out], [gain]],
            after=[token], scratch=[VMEM((rows, width), BF16), DMA((6,))],
        )
        return out, out[1]

    k, v = [], []

    def own_state(sent):
        out = make_state(0, [sent])
        k.extend(held["k", i] for i in range(2))
        v.extend(held["v", i] for i in range(2))
        return out

    own, other, work = carry(own_state, lambda: make_state(1), CHUNKS, False, local_work)
    scores, part, q, weighted, gain = work
    attended, carried, stats = [], [], []
    for which, came in enumerate((own, other)):
        out = call(
            attend_kernel, [which, CHUNKS], [half, ((part_width, HD), BF16), sums],
            [row, q, part, weighted, *came, *stats[-1:]],
        )
        for kept, new in zip((attended, carried, stats), out):
            kept.append(new)
    stats = stats[-1:]
    stats += [
        lax.ppermute(stats[0], "head", [(i, (i + apart) % ranks) for i in range(ranks)])
        for apart in range(1, ranks)
    ]

    def make_grad(which, after=()):
        held["g", which], out = call(
            grad_kernel, [which, ranks], [half, state],
            [row, q, weighted, attended[which], *stats], after=after,
        )
        return out

    def back_work(token):
        out = call(
            back_kernel, [ranks], [((rows, width), BF16, HBM)] * 2 + [wide, wide],
            [row, q, scores, gain, *k, *v, held["g", 0], held["g", 1], *attended, *carried, *stats],
            after=[token],
            scratch=[VMEM((rows, width), BF16), VMEM((rows, width), BF16), DMA((4,))],
        )
        return out, out[2]

    own, other, work = carry(
        lambda sent: make_grad(0, [sent]), lambda: make_grad(1), CHUNKS, True, back_work
    )
    normed, grad_q, part_k, part_v = work
    done = ()
    for which, came in enumerate((own, other)):
        n = 5 + CHUNKS
        done = call(
            last_kernel, [which, CHUNKS], [((rows, width), BF16, HBM)] * 2,
            [row, k[which], v[which], part_k, part_v, *came], after=done,
            scratch=[VMEM(*half), VMEM(*half), DMA((heads,))],
            aliases={n: 0, n + 1: 1} if done else {},
        )
    return normed, grad_q, *done


def solution(mesh):
    cut = P("ctx", "head")
    return jax.shard_map(
        local,
        mesh=mesh,
        in_specs=(cut, cut, cut, cut, P("ctx"), P("head")),
        out_specs=(cut, cut, cut, cut),
        check_vma=False,
    )
```

```python
import jax
import jax.numpy as jnp
from jax import lax
from jax.experimental import pallas as pl
from jax.experimental.pallas import tpu as pltpu
from jax.sharding import PartitionSpec as P

HEADS = 32
HD = 128
TAG = 8
F32 = jnp.float32
BF16 = jnp.bfloat16
VMEM, HBM, ANY = pltpu.VMEM, pltpu.HBM, pl.ANY
DMA = pltpu.SemaphoreType.DMA
NN = ((1,), (0,))
NT = ((1,), (1,))
TN = ((0,), (0,))


def dot(a, b, dims):
    return lax.dot_general(a, b, (dims, ((), ())), preferred_element_type=F32)


def head(h):
    return slice(h * HD, (h + 1) * HD)


def core():
    return lax.rem(lax.axis_index("ctx"), 2)


def columns(half, width):
    at = core() if half == 0 else 1 - core()
    return pl.ds(pl.multiple_of(at * width, width), width)


def as_column(row):
    return jnp.transpose(jnp.broadcast_to(row, (HD, row.shape[1])))


def in_doc(row_ref, at):
    row = row_ref[...].astype(F32)
    which = jnp.broadcast_to(row[:, at:at + 1], (row.shape[1], HD))
    return (as_column(row) == which).astype(F32)


def tag(row_ref, at):
    return jnp.broadcast_to(row_ref[:, at:at + 1].astype(F32), (1, HD))


def visible(row_ref):
    rows = row_ref.shape[1]
    row = row_ref[...].astype(F32)
    column = as_column(row)
    column = jnp.concatenate([column] * (rows // HD), axis=1)
    t = lax.broadcasted_iota(jnp.int32, (rows, rows), 0)
    s = lax.broadcasted_iota(jnp.int32, (rows, rows), 1)
    return (column == jnp.broadcast_to(row, (rows, rows))) & (t >= s)


def state_kernel(half, row, k_hbm, v_hbm, *rest):
    if half:
        out, k, v, row_out, sems = rest[-5:]
    else:
        out, k, v, sems = rest[-4:]
    rows, width = k.shape
    span = columns(half, width)
    copies = [
        pltpu.make_async_copy(k_hbm.at[:, span], k, sems.at[1]),
        pltpu.make_async_copy(v_hbm.at[:, span], v, sems.at[2]),
    ]
    if half:
        copies.insert(0, pltpu.make_async_copy(row, row_out, sems.at[0]))
        row = row_out
    for copy in copies:
        copy.start()
    if half:
        copies.pop(0).wait()
    keep = in_doc(row, rows - 1).astype(BF16)
    out[width:, :] = jnp.broadcast_to(tag(row, rows - 1), (TAG, HD))
    for copy in copies:
        copy.wait()
    for h in range(width // HD):
        out[head(h), :] = dot(k[:, head(h)] * keep, v[:, head(h)], TN)


def add_into(out, near, far, near_lo, far_lo):
    size = out.shape[0] - TAG
    near_tag = near[near.shape[0] - TAG:, :]
    same = near_tag[0:1, :] == far[far.shape[0] - TAG:far.shape[0] - TAG + 1, :]
    here = far[far_lo:far_lo + size, :]
    out[:size, :] = near[near_lo:near_lo + size, :] + jnp.where(same, here, 0.0)
    out[size:, :] = near_tag


def pair_kernel(backward, mine, came, *outs):
    size = outs[0].shape[0] - TAG
    upstream = core() == int(backward)

    def fill(down, up):
        for i, out in enumerate(outs):
            add_into(out, down, up, i * size, i * size)

    pl.when(upstream)(lambda: fill(came, mine))
    pl.when(jnp.logical_not(upstream))(lambda: fill(mine, came))


def merge_kernel(near, far, *rest):
    add_into(rest[-1], near, far, 0, 0)


def split_kernel(backward, part, entering, mine, came, keep, send):
    size = entering.shape[0] - TAG
    upstream = core() == int(backward)

    def fill(to_up, to_down, up):
        to_up[...] = entering[...]
        add_into(to_down, up, entering, part * size, 0)

    pl.when(upstream)(lambda: fill(keep, send, mine))
    pl.when(jnp.logical_not(upstream))(lambda: fill(send, keep, came))


def local_kernel(row, k0, k1, v0, v1, q_hbm, grad_hbm, gain_hbm, *rest):
    scores, part, q, weighted, gain, grad, sems = rest[-7:]
    rows, width = k0.shape
    copies = []
    for i, (hbm, held) in enumerate(((q_hbm, q), (gain_hbm, gain), (grad_hbm, grad))):
        for half in range(2):
            at = slice(half * width, (half + 1) * width)
            copies.append(
                pltpu.make_async_copy(
                    hbm.at[:, columns(half, width)], held.at[:, at], sems.at[2 * i + half]
                )
            )
            copies[-1].start()
    seen = visible(row)
    copies[0].wait()
    copies[1].wait()
    n = width // HD
    for h in range(2 * n):
        k, v = (k0, v0) if h < n else (k1, v1)
        sc = dot(q[:, head(h)], k[:, head(h % n)], NT)
        sc = jnp.where(seen, sc, 0.0).astype(BF16)
        scores[h] = sc
        part[:, head(h)] = dot(sc, v[:, head(h % n)], NN)
    for copy in copies[2:]:
        copy.wait()
    for h in range(2 * n):
        weighted[:, head(h)] = gain[:, head(h)] * grad[:, head(h)].astype(F32)


def pieces(refs):
    for ref in refs:
        size = ref.shape[0] - TAG
        for h in range(size // HD):
            yield ref[head(h), :], ref[size:size + 1, :]


def attend_kernel(half, chunks, row, q, part, weighted, *rest):
    came, rest = rest[:chunks], rest[chunks:]
    attended, carried, stats = rest[-3:]
    rows, width = attended.shape
    keep = in_doc(row, 0)
    first = tag(row, 0)
    square = jnp.zeros((rows, HD), F32)
    inner = jnp.zeros((rows, HD), F32)
    for h, (state, its) in enumerate(pieces(came)):
        at = head(half * (width // HD) + h)
        state = jnp.where(its == first, state, 0.0).astype(BF16)
        carried[head(h), :] = state
        att = (part[:, at] + keep * dot(q[:, at], state, NN)).astype(BF16)
        attended[:, head(h)] = att
        att = att.astype(F32)
        square = square + att * att
        inner = inner + weighted[:, at] * att
    ones = jnp.ones((TAG, HD), F32)
    upper = lax.broadcasted_iota(jnp.int32, (TAG, rows), 0) < TAG // 2
    exact = lax.Precision.HIGHEST
    sums = [
        lax.dot_general(ones, x, (NT, ((), ())), precision=exact, preferred_element_type=F32)
        for x in (square, inner)
    ]
    sums = jnp.where(upper, sums[0], sums[1])
    stats[...] = sums + rest[0][...] if len(rest) > 3 else sums


def norm_scales(parts):
    feats = HEADS * HD
    total = parts[0][...]
    for x in parts[1:]:
        total = total + x[...]
    inv = lax.rsqrt(total[0:1, :] / feats + 1e-06)
    back = inv * inv * inv * (total[TAG - 1:TAG, :] / feats)
    return as_column(inv), as_column(back)


def grad_kernel(half, ranks, row, q, weighted, attended, *rest):
    g_out, out = rest[-2:]
    rows, width = attended.shape
    keep = in_doc(row, 0).astype(BF16)
    inv, back = norm_scales(rest[:ranks])
    for h in range(width // HD):
        at = head(half * (width // HD) + h)
        g = (inv * weighted[:, at] - attended[:, head(h)].astype(F32) * back).astype(BF16)
        g_out[:, head(h)] = g
        out[head(h), :] = dot(q[:, at] * keep, g, TN)
    out[width:, :] = jnp.broadcast_to(tag(row, 0), (TAG, HD))


def back_kernel(ranks, row, q, scores, gain, k0, k1, v0, v1, g0, g1, a0, a1, c0, c1, *rest):
    normed_hbm, grad_q_hbm, part_k, part_v, normed, grad_q, sems = rest[-7:]
    rows, width = k0.shape
    inv, _ = norm_scales(rest[:ranks])
    keep = in_doc(row, 0)
    seen = visible(row)
    n = width // HD
    copies = []
    for half, (k, v, g, attended, carried) in enumerate(((k0, v0, g0, a0, c0), (k1, v1, g1, a1, c1))):
        for h in range(n):
            at = head(half * n + h)
            gh = g[:, head(h)]
            normed[:, at] = (gain[:, at] * attended[:, head(h)].astype(F32) * inv).astype(BF16)
            gs = dot(gh, v[:, head(h)], NT)
            gs = jnp.where(seen, gs, 0.0).astype(BF16)
            whole = dot(gs, k[:, head(h)], NN) + keep * dot(gh, carried[head(h), :], NT)
            grad_q[:, at] = whole.astype(BF16)
            part_k[:, at] = dot(gs, q[:, at], TN)
            part_v[:, at] = dot(scores[half * n + h], gh, TN)
        span = slice(half * width, (half + 1) * width)
        for i, (held, out) in enumerate(((normed, normed_hbm), (grad_q, grad_q_hbm))):
            copies.append(
                pltpu.make_async_copy(
                    held.at[:, span], out.at[:, columns(half, width)], sems.at[2 * half + i]
                )
            )
            copies[-1].start()
    for copy in copies:
        copy.wait()


def last_kernel(half, chunks, row, k, v, part_k, part_v, *rest):
    came = rest[:chunks]
    k_hbm, v_hbm, grad_k, grad_v, sems = rest[-5:]
    rows, width = k.shape
    keep = in_doc(row, rows - 1)
    last = tag(row, rows - 1)
    at_core = core() if half == 0 else 1 - core()
    copies = []
    for h, (state, its) in enumerate(pieces(came)):
        at = head(half * (width // HD) + h)
        later = jnp.where(its == last, state, 0.0).astype(BF16)
        grad_k[:, head(h)] = (part_k[:, at] + keep * dot(v[:, head(h)], later, NT)).astype(BF16)
        grad_v[:, head(h)] = (part_v[:, at] + keep * dot(k[:, head(h)], later, NN)).astype(BF16)
        span = pl.ds(pl.multiple_of(at_core * width + h * HD, HD), HD)
        for i, (held, out) in enumerate(((grad_k, k_hbm), (grad_v, v_hbm))):
            copies.append(
                pltpu.make_async_copy(held.at[:, head(h)], out.at[:, span], sems.at[2 * h + i])
            )
            copies[-1].start()
    for copy in copies:
        copy.wait()


def call(kernel, fixed, outs, args, after=(), scratch=(), aliases={}):
    spaces = [HBM if isinstance(x, list) else VMEM for x in args] + [ANY] * len(after)
    args = [
        pltpu.with_memory_space_constraint(x[0], HBM) if isinstance(x, list) else x for x in args
    ]
    return pl.pallas_call(
        lambda *refs: kernel(*fixed, *refs),
        out_shape=[jax.ShapeDtypeStruct(*out[:2]) for out in outs],
        in_specs=[pl.BlockSpec(memory_space=space) for space in spaces],
        out_specs=[pl.BlockSpec(memory_space=(*out, VMEM)[2]) for out in outs],
        scratch_shapes=scratch,
        input_output_aliases=aliases,
        compiler_params=pltpu.CompilerParams(vmem_limit_bytes=40 * 1024 * 1024),
        name=kernel.__name__[:-7],
    )(*args, *after)


def carry(mine, other, chunks, backward, beside):
    blocks = lax.axis_size("ctx")
    step = -2 if backward else 2

    def swap(value):
        return lax.ppermute(value, "ctx", [(i, i ^ 1) for i in range(blocks)])

    def hop(value):
        pairs = [(i, i + step) for i in range(blocks) if 0 <= i + step < blocks]
        return lax.ppermute(value, "ctx", pairs)

    sent = other()
    came = swap(sent)
    mine = mine(sent)
    size = (mine.shape[0] - TAG) // chunks
    chunk = ((size + TAG, HD), F32)
    both = call(pair_kernel, [backward], [chunk] * chunks, [mine, came])
    once = [hop(b) for b in both]
    work, token = beside(both[-1])
    window = [call(merge_kernel, [], [chunk], [b, o], [token])[0] for b, o in zip(both, once)]
    entering = [hop(w) for w in window]
    keep, back = [], []
    for i, e in enumerate(entering):
        kept, send = call(split_kernel, [backward, i], [chunk] * 2, [e, mine, came])
        keep.append(kept)
        back.append(swap(send))
    return keep, back, work


CHUNKS = 2


def local(queries, key_rows, value_rows, grad_out, doc_ids, out_gain):
    rows, width = queries.shape
    heads = width // HD
    part_width = width // 2
    ranks = lax.axis_size("head")
    ids = doc_ids.reshape(1, rows)
    gain = out_gain.reshape(1, width)
    wide, half, sums = ((rows, width), F32), ((rows, part_width), BF16), ((TAG, rows), F32)
    state = ((part_width + TAG, HD), F32)

    held = {}

    def make_state(which, after=()):
        out, held["k", which], held["v", which], *row = call(
            state_kernel, [which], [state, half, half] + [((1, rows), jnp.int32)] * which,
            [[ids] if which else held["row"], [key_rows], [value_rows]],
            after=after, scratch=[DMA((3,))],
        )
        if which:
            (held["row"],) = row
        return out

    def local_work(token):
        out = call(
            local_kernel, [],
            [((heads, rows, rows), BF16), wide, ((rows, width), BF16), wide, ((1, width), F32)],
            [held["row"], *k, *v, [queries], [grad_out], [gain]],
            after=[token], scratch=[VMEM((rows, width), BF16), DMA((6,))],
        )
        return out, out[1]

    k, v = [], []

    def own_state(sent):
        out = make_state(0, [sent])
        k.extend(held["k", i] for i in range(2))
        v.extend(held["v", i] for i in range(2))
        return out

    own, other, work = carry(own_state, lambda: make_state(1), CHUNKS, False, local_work)
    scores, part, q, weighted, gain = work
    attended, carried, stats = [], [], []
    for which, came in enumerate((own, other)):
        out = call(
            attend_kernel, [which, CHUNKS], [half, ((part_width, HD), BF16), sums],
            [held["row"], q, part, weighted, *came, *stats[-1:]],
        )
        for kept, new in zip((attended, carried, stats), out):
            kept.append(new)
    stats = stats[-1:]
    stats += [
        lax.ppermute(stats[0], "head", [(i, (i + apart) % ranks) for i in range(ranks)])
        for apart in range(1, ranks)
    ]

    def make_grad(which, after=()):
        held["g", which], out = call(
            grad_kernel, [which, ranks], [half, state],
            [held["row"], q, weighted, attended[which], *stats], after=after,
        )
        return out

    def back_work(token):
        out = call(
            back_kernel, [ranks], [((rows, width), BF16, HBM)] * 2 + [wide, wide],
            [held["row"], q, scores, gain, *k, *v, held["g", 0], held["g", 1], *attended, *carried, *stats],
            after=[token],
            scratch=[VMEM((rows, width), BF16), VMEM((rows, width), BF16), DMA((4,))],
        )
        return out, out[2]

    own, other, work = carry(
        lambda sent: make_grad(0, [sent]), lambda: make_grad(1), CHUNKS, True, back_work
    )
    normed, grad_q, part_k, part_v = work
    done = ()
    for which, came in enumerate((own, other)):
        n = 5 + CHUNKS
        done = call(
            last_kernel, [which, CHUNKS], [((rows, width), BF16, HBM)] * 2,
            [held["row"], k[which], v[which], part_k, part_v, *came], after=done,
            scratch=[VMEM(*half), VMEM(*half), DMA((heads,))],
            aliases={n: 0, n + 1: 1} if done else {},
        )
    return normed, grad_q, *done


def solution(mesh):
    cut = P("ctx", "head")
    return jax.shard_map(
        local,
        mesh=mesh,
        in_specs=(cut, cut, cut, cut, P("ctx"), P("head")),
        out_specs=(cut, cut, cut, cut),
        check_vma=False,
    )
```

```python
import jax
import jax.numpy as jnp
from jax import lax
from jax.experimental import pallas as pl
from jax.experimental.pallas import tpu as pltpu
from jax.sharding import PartitionSpec as P

HEADS = 32
HD = 128
TAG = 8
F32 = jnp.float32
BF16 = jnp.bfloat16
VMEM, HBM, ANY = pltpu.VMEM, pltpu.HBM, pl.ANY
DMA = pltpu.SemaphoreType.DMA
NN = ((1,), (0,))
NT = ((1,), (1,))
TN = ((0,), (0,))


def dot(a, b, dims):
    return lax.dot_general(a, b, (dims, ((), ())), preferred_element_type=F32)


def head(h):
    return slice(h * HD, (h + 1) * HD)


def core():
    return lax.rem(lax.axis_index("ctx"), 2)


def columns(half, width):
    at = core() if half == 0 else 1 - core()
    return pl.ds(pl.multiple_of(at * width, width), width)


def as_column(row):
    return jnp.transpose(jnp.broadcast_to(row, (HD, row.shape[1])))


def in_doc(row_ref, at):
    row = row_ref[...].astype(F32)
    which = jnp.broadcast_to(row[:, at:at + 1], (row.shape[1], HD))
    return (as_column(row) == which).astype(F32)


def tag(row_ref, at):
    return jnp.broadcast_to(row_ref[:, at:at + 1].astype(F32), (1, HD))


def visible(row_ref):
    rows = row_ref.shape[1]
    row = row_ref[...].astype(F32)
    column = as_column(row)
    column = jnp.concatenate([column] * (rows // HD), axis=1)
    t = lax.broadcasted_iota(jnp.int32, (rows, rows), 0)
    s = lax.broadcasted_iota(jnp.int32, (rows, rows), 1)
    return (column == jnp.broadcast_to(row, (rows, rows))) & (t >= s)


def state_kernel(half, row, k_hbm, v_hbm, *rest):
    if half:
        out, k, v, row_out, sems = rest[-5:]
    else:
        out, k, v, sems = rest[-4:]
    rows, width = k.shape
    n = width // HD
    at_core = core() if half == 0 else 1 - core()
    copies = []
    if half:
        copies.append(pltpu.make_async_copy(row, row_out, sems.at[2 * n]))
        row = row_out
    for h in range(n):
        span = pl.ds(pl.multiple_of(at_core * width + h * HD, HD), HD)
        for i, (hbm, held) in enumerate(((k_hbm, k), (v_hbm, v))):
            copies.append(
                pltpu.make_async_copy(hbm.at[:, span], held.at[:, head(h)], sems.at[2 * h + i])
            )
    for copy in copies:
        copy.start()
    if half:
        copies.pop(0).wait()
    keep = in_doc(row, rows - 1).astype(BF16)
    out[width:, :] = jnp.broadcast_to(tag(row, rows - 1), (TAG, HD))
    for h in range(n):
        copies[2 * h].wait()
        copies[2 * h + 1].wait()
        out[head(h), :] = dot(k[:, head(h)] * keep, v[:, head(h)], TN)


def add_into(out, near, far, near_lo, far_lo):
    size = out.shape[0] - TAG
    near_tag = near[near.shape[0] - TAG:, :]
    same = near_tag[0:1, :] == far[far.shape[0] - TAG:far.shape[0] - TAG + 1, :]
    here = far[far_lo:far_lo + size, :]
    out[:size, :] = near[near_lo:near_lo + size, :] + jnp.where(same, here, 0.0)
    out[size:, :] = near_tag


def pair_kernel(backward, mine, came, *outs):
    size = outs[0].shape[0] - TAG
    upstream = core() == int(backward)

    def fill(down, up):
        for i, out in enumerate(outs):
            add_into(out, down, up, i * size, i * size)

    pl.when(upstream)(lambda: fill(came, mine))
    pl.when(jnp.logical_not(upstream))(lambda: fill(mine, came))


def merge_kernel(near, far, *rest):
    add_into(rest[-1], near, far, 0, 0)


def split_kernel(backward, part, entering, mine, came, keep, send):
    size = entering.shape[0] - TAG
    upstream = core() == int(backward)

    def fill(to_up, to_down, up):
        to_up[...] = entering[...]
        add_into(to_down, up, entering, part * size, 0)

    pl.when(upstream)(lambda: fill(keep, send, mine))
    pl.when(jnp.logical_not(upstream))(lambda: fill(send, keep, came))


def local_kernel(row, k0, k1, v0, v1, q_hbm, grad_hbm, gain_hbm, *rest):
    scores, part, q, weighted, gain, grad, sems = rest[-7:]
    rows, width = k0.shape
    copies = []
    for i, (hbm, held) in enumerate(((q_hbm, q), (gain_hbm, gain), (grad_hbm, grad))):
        for half in range(2):
            at = slice(half * width, (half + 1) * width)
            copies.append(
                pltpu.make_async_copy(
                    hbm.at[:, columns(half, width)], held.at[:, at], sems.at[2 * i + half]
                )
            )
            copies[-1].start()
    seen = visible(row)
    copies[0].wait()
    copies[1].wait()
    n = width // HD
    for h in range(2 * n):
        k, v = (k0, v0) if h < n else (k1, v1)
        sc = dot(q[:, head(h)], k[:, head(h % n)], NT)
        sc = jnp.where(seen, sc, 0.0).astype(BF16)
        scores[h] = sc
        part[:, head(h)] = dot(sc, v[:, head(h % n)], NN)
    for copy in copies[2:]:
        copy.wait()
    for h in range(2 * n):
        weighted[:, head(h)] = gain[:, head(h)] * grad[:, head(h)].astype(F32)


def pieces(refs):
    for ref in refs:
        size = ref.shape[0] - TAG
        for h in range(size // HD):
            yield ref[head(h), :], ref[size:size + 1, :]


def attend_kernel(half, chunks, row, q, part, weighted, *rest):
    came, rest = rest[:chunks], rest[chunks:]
    attended, carried, stats = rest[-3:]
    rows, width = attended.shape
    keep = in_doc(row, 0)
    first = tag(row, 0)
    square = jnp.zeros((rows, HD), F32)
    inner = jnp.zeros((rows, HD), F32)
    for h, (state, its) in enumerate(pieces(came)):
        at = head(half * (width // HD) + h)
        state = jnp.where(its == first, state, 0.0).astype(BF16)
        carried[head(h), :] = state
        att = (part[:, at] + keep * dot(q[:, at], state, NN)).astype(BF16)
        attended[:, head(h)] = att
        att = att.astype(F32)
        square = square + att * att
        inner = inner + weighted[:, at] * att
    ones = jnp.ones((TAG, HD), F32)
    upper = lax.broadcasted_iota(jnp.int32, (TAG, rows), 0) < TAG // 2
    exact = lax.Precision.HIGHEST
    sums = [
        lax.dot_general(ones, x, (NT, ((), ())), precision=exact, preferred_element_type=F32)
        for x in (square, inner)
    ]
    sums = jnp.where(upper, sums[0], sums[1])
    stats[...] = sums + rest[0][...] if len(rest) > 3 else sums


def norm_scales(parts):
    feats = HEADS * HD
    total = parts[0][...]
    for x in parts[1:]:
        total = total + x[...]
    inv = lax.rsqrt(total[0:1, :] / feats + 1e-06)
    back = inv * inv * inv * (total[TAG - 1:TAG, :] / feats)
    return as_column(inv), as_column(back)


def grad_kernel(half, ranks, row, q, weighted, attended, *rest):
    g_out, out = rest[-2:]
    rows, width = attended.shape
    keep = in_doc(row, 0).astype(BF16)
    inv, back = norm_scales(rest[:ranks])
    for h in range(width // HD):
        at = head(half * (width // HD) + h)
        g = (inv * weighted[:, at] - attended[:, head(h)].astype(F32) * back).astype(BF16)
        g_out[:, head(h)] = g
        out[head(h), :] = dot(q[:, at] * keep, g, TN)
    out[width:, :] = jnp.broadcast_to(tag(row, 0), (TAG, HD))


def back_kernel(ranks, row, q, scores, gain, k0, k1, v0, v1, g0, g1, a0, a1, c0, c1, *rest):
    normed_hbm, grad_q_hbm, part_k, part_v, normed, grad_q, sems = rest[-7:]
    rows, width = k0.shape
    inv, _ = norm_scales(rest[:ranks])
    keep = in_doc(row, 0)
    seen = visible(row)
    n = width // HD
    copies = []
    for half, (k, v, g, attended, carried) in enumerate(((k0, v0, g0, a0, c0), (k1, v1, g1, a1, c1))):
        for h in range(n):
            at = head(half * n + h)
            gh = g[:, head(h)]
            normed[:, at] = (gain[:, at] * attended[:, head(h)].astype(F32) * inv).astype(BF16)
            gs = dot(gh, v[:, head(h)], NT)
            gs = jnp.where(seen, gs, 0.0).astype(BF16)
            whole = dot(gs, k[:, head(h)], NN) + keep * dot(gh, carried[head(h), :], NT)
            grad_q[:, at] = whole.astype(BF16)
            part_k[:, at] = dot(gs, q[:, at], TN)
            part_v[:, at] = dot(scores[half * n + h], gh, TN)
        span = slice(half * width, (half + 1) * width)
        for i, (held, out) in enumerate(((normed, normed_hbm), (grad_q, grad_q_hbm))):
            copies.append(
                pltpu.make_async_copy(
                    held.at[:, span], out.at[:, columns(half, width)], sems.at[2 * half + i]
                )
            )
            copies[-1].start()
    for copy in copies:
        copy.wait()


def last_kernel(half, chunks, row, k, v, part_k, part_v, *rest):
    came = rest[:chunks]
    k_hbm, v_hbm, grad_k, grad_v, sems = rest[-5:]
    rows, width = k.shape
    keep = in_doc(row, rows - 1)
    last = tag(row, rows - 1)
    at_core = core() if half == 0 else 1 - core()
    copies = []
    for h, (state, its) in enumerate(pieces(came)):
        at = head(half * (width // HD) + h)
        later = jnp.where(its == last, state, 0.0).astype(BF16)
        grad_k[:, head(h)] = (part_k[:, at] + keep * dot(v[:, head(h)], later, NT)).astype(BF16)
        grad_v[:, head(h)] = (part_v[:, at] + keep * dot(k[:, head(h)], later, NN)).astype(BF16)
        span = pl.ds(pl.multiple_of(at_core * width + h * HD, HD), HD)
        for i, (held, out) in enumerate(((grad_k, k_hbm), (grad_v, v_hbm))):
            copies.append(
                pltpu.make_async_copy(held.at[:, head(h)], out.at[:, span], sems.at[2 * h + i])
            )
            copies[-1].start()
    for copy in copies:
        copy.wait()


def call(kernel, fixed, outs, args, after=(), scratch=(), aliases={}):
    spaces = [HBM if isinstance(x, list) else VMEM for x in args] + [ANY] * len(after)
    args = [
        pltpu.with_memory_space_constraint(x[0], HBM) if isinstance(x, list) else x for x in args
    ]
    return pl.pallas_call(
        lambda *refs: kernel(*fixed, *refs),
        out_shape=[jax.ShapeDtypeStruct(*out[:2]) for out in outs],
        in_specs=[pl.BlockSpec(memory_space=space) for space in spaces],
        out_specs=[pl.BlockSpec(memory_space=(*out, VMEM)[2]) for out in outs],
        scratch_shapes=scratch,
        input_output_aliases=aliases,
        compiler_params=pltpu.CompilerParams(vmem_limit_bytes=40 * 1024 * 1024),
        name=kernel.__name__[:-7],
    )(*args, *after)


def carry(mine, other, chunks, backward, beside):
    blocks = lax.axis_size("ctx")
    step = -2 if backward else 2

    def swap(value):
        return lax.ppermute(value, "ctx", [(i, i ^ 1) for i in range(blocks)])

    def hop(value):
        return lax.ppermute(value, "ctx", [(i, (i + step) % blocks) for i in range(blocks)])

    sent = other()
    came = swap(sent)
    mine = mine(sent)
    size = (mine.shape[0] - TAG) // chunks
    chunk = ((size + TAG, HD), F32)
    both = call(pair_kernel, [backward], [chunk] * chunks, [mine, came])
    once = [hop(b) for b in both]
    work, token = beside(both[-1])
    window = [call(merge_kernel, [], [chunk], [b, o], [token])[0] for b, o in zip(both, once)]
    entering = [hop(w) for w in window]
    keep, back = [], []
    for i, e in enumerate(entering):
        kept, send = call(split_kernel, [backward, i], [chunk] * 2, [e, mine, came])
        keep.append(kept)
        back.append(swap(send))
    return keep, back, work


CHUNKS = 1


def local(queries, key_rows, value_rows, grad_out, doc_ids, out_gain):
    rows, width = queries.shape
    heads = width // HD
    part_width = width // 2
    ranks = lax.axis_size("head")
    ids = doc_ids.reshape(1, rows)
    gain = out_gain.reshape(1, width)
    wide, half, sums = ((rows, width), F32), ((rows, part_width), BF16), ((TAG, rows), F32)
    state = ((part_width + TAG, HD), F32)

    held = {}

    def make_state(which, after=()):
        out, held["k", which], held["v", which], *row = call(
            state_kernel, [which], [state, half, half] + [((1, rows), jnp.int32)] * which,
            [[ids] if which else held["row"], [key_rows], [value_rows]],
            after=after, scratch=[DMA((heads + 1,))],
        )
        if which:
            (held["row"],) = row
        return out

    def local_work(token):
        out = call(
            local_kernel, [],
            [((heads, rows, rows), BF16), wide, ((rows, width), BF16), wide, ((1, width), F32)],
            [held["row"], *k, *v, [queries], [grad_out], [gain]],
            after=[token], scratch=[VMEM((rows, width), BF16), DMA((6,))],
        )
        return out, out[1]

    k, v = [], []

    def own_state(sent):
        out = make_state(0, [sent])
        k.extend(held["k", i] for i in range(2))
        v.extend(held["v", i] for i in range(2))
        return out

    own, other, work = carry(own_state, lambda: make_state(1), CHUNKS, False, local_work)
    scores, part, q, weighted, gain = work
    attended, carried, stats = [], [], []
    for which, came in enumerate((own, other)):
        out = call(
            attend_kernel, [which, CHUNKS], [half, ((part_width, HD), BF16), sums],
            [held["row"], q, part, weighted, *came, *stats[-1:]],
        )
        for kept, new in zip((attended, carried, stats), out):
            kept.append(new)
    stats = stats[-1:]
    stats += [
        lax.ppermute(stats[0], "head", [(i, (i + apart) % ranks) for i in range(ranks)])
        for apart in range(1, ranks)
    ]

    def make_grad(which, after=()):
        held["g", which], out = call(
            grad_kernel, [which, ranks], [half, state],
            [held["row"], q, weighted, attended[which], *stats], after=after,
        )
        return out

    def back_work(token):
        out = call(
            back_kernel, [ranks], [((rows, width), BF16, HBM)] * 2 + [wide, wide],
            [held["row"], q, scores, gain, *k, *v, held["g", 0], held["g", 1], *attended, *carried, *stats],
            after=[token],
            scratch=[VMEM((rows, width), BF16), VMEM((rows, width), BF16), DMA((4,))],
        )
        return out, out[2]

    own, other, work = carry(
        lambda sent: make_grad(0, [sent]), lambda: make_grad(1), CHUNKS, True, back_work
    )
    normed, grad_q, part_k, part_v = work
    done = ()
    for which, came in enumerate((own, other)):
        n = 5 + CHUNKS
        done = call(
            last_kernel, [which, CHUNKS], [((rows, width), BF16, HBM)] * 2,
            [held["row"], k[which], v[which], part_k, part_v, *came], after=done,
            scratch=[VMEM(*half), VMEM(*half), DMA((heads,))],
            aliases={n: 0, n + 1: 1} if done else {},
        )
    return normed, grad_q, *done


def solution(mesh):
    cut = P("ctx", "head")
    return jax.shard_map(
        local,
        mesh=mesh,
        in_specs=(cut, cut, cut, cut, P("ctx"), P("head")),
        out_specs=(cut, cut, cut, cut),
        check_vma=False,
    )
```

```python
import jax
import jax.numpy as jnp
from jax import lax
from jax.experimental import pallas as pl
from jax.experimental.pallas import tpu as pltpu
from jax.sharding import PartitionSpec as P

HEADS = 32
HD = 128
TAG = 8
F32 = jnp.float32
BF16 = jnp.bfloat16
VMEM, HBM, ANY = pltpu.VMEM, pltpu.HBM, pl.ANY
DMA = pltpu.SemaphoreType.DMA
NN = ((1,), (0,))
NT = ((1,), (1,))
TN = ((0,), (0,))


def dot(a, b, dims):
    return lax.dot_general(a, b, (dims, ((), ())), preferred_element_type=F32)


def head(h):
    return slice(h * HD, (h + 1) * HD)


def core():
    return lax.rem(lax.axis_index("ctx"), 2)


def columns(half, width):
    at = core() if half == 0 else 1 - core()
    return pl.ds(pl.multiple_of(at * width, width), width)


def as_column(row):
    return jnp.transpose(jnp.broadcast_to(row, (HD, row.shape[1])))


def in_doc(row_ref, at):
    row = row_ref[...].astype(F32)
    which = jnp.broadcast_to(row[:, at:at + 1], (row.shape[1], HD))
    return (as_column(row) == which).astype(F32)


def tag(row_ref, at):
    return jnp.broadcast_to(row_ref[:, at:at + 1].astype(F32), (1, HD))


def visible(row_ref):
    rows = row_ref.shape[1]
    row = row_ref[...].astype(F32)
    column = as_column(row)
    column = jnp.concatenate([column] * (rows // HD), axis=1)
    t = lax.broadcasted_iota(jnp.int32, (rows, rows), 0)
    s = lax.broadcasted_iota(jnp.int32, (rows, rows), 1)
    return (column == jnp.broadcast_to(row, (rows, rows))) & (t >= s)


def state_kernel(half, row, k_hbm, v_hbm, *rest):
    if half:
        out, k, v, row_out, sems = rest[-5:]
    else:
        out, k, v, sems = rest[-4:]
    rows, width = k.shape
    span = columns(half, width)
    copies = [
        pltpu.make_async_copy(k_hbm.at[:, span], k, sems.at[1]),
        pltpu.make_async_copy(v_hbm.at[:, span], v, sems.at[2]),
    ]
    if half:
        copies.insert(0, pltpu.make_async_copy(row, row_out, sems.at[0]))
        row = row_out
    for copy in copies:
        copy.start()
    if half:
        copies.pop(0).wait()
    keep = in_doc(row, rows - 1).astype(BF16)
    out[width:, :] = jnp.broadcast_to(tag(row, rows - 1), (TAG, HD))
    for copy in copies:
        copy.wait()
    for h in range(width // HD):
        out[head(h), :] = dot(k[:, head(h)] * keep, v[:, head(h)], TN)


def add_into(out, near, far, near_lo, far_lo):
    size = out.shape[0] - TAG
    near_tag = near[near.shape[0] - TAG:, :]
    same = near_tag[0:1, :] == far[far.shape[0] - TAG:far.shape[0] - TAG + 1, :]
    here = far[far_lo:far_lo + size, :]
    out[:size, :] = near[near_lo:near_lo + size, :] + jnp.where(same, here, 0.0)
    out[size:, :] = near_tag


def pair_kernel(backward, mine, came, *outs):
    size = outs[0].shape[0] - TAG
    upstream = core() == int(backward)

    def fill(down, up):
        for i, out in enumerate(outs):
            add_into(out, down, up, i * size, i * size)

    pl.when(upstream)(lambda: fill(came, mine))
    pl.when(jnp.logical_not(upstream))(lambda: fill(mine, came))


def merge_kernel(near, far, *rest):
    add_into(rest[-1], near, far, 0, 0)


def split_kernel(backward, part, entering, mine, came, *rest):
    keep, send = rest[-2:]
    size = entering.shape[0] - TAG
    upstream = core() == int(backward)

    def fill(to_up, to_down, up):
        to_up[...] = entering[...]
        add_into(to_down, up, entering, part * size, 0)

    pl.when(upstream)(lambda: fill(keep, send, mine))
    pl.when(jnp.logical_not(upstream))(lambda: fill(send, keep, came))


def local_kernel(row, k0, k1, v0, v1, q_hbm, grad_hbm, gain_hbm, *rest):
    scores, part, q, weighted, gain, grad, sems = rest[-7:]
    rows, width = k0.shape
    copies = []
    for i, (hbm, held) in enumerate(((q_hbm, q), (gain_hbm, gain), (grad_hbm, grad))):
        for half in range(2):
            at = slice(half * width, (half + 1) * width)
            copies.append(
                pltpu.make_async_copy(
                    hbm.at[:, columns(half, width)], held.at[:, at], sems.at[2 * i + half]
                )
            )
            copies[-1].start()
    seen = visible(row)
    copies[0].wait()
    copies[1].wait()
    n = width // HD
    for h in range(2 * n):
        k, v = (k0, v0) if h < n else (k1, v1)
        sc = dot(q[:, head(h)], k[:, head(h % n)], NT)
        sc = jnp.where(seen, sc, 0.0).astype(BF16)
        scores[h] = sc
        part[:, head(h)] = dot(sc, v[:, head(h % n)], NN)
    for copy in copies[2:]:
        copy.wait()
    for h in range(2 * n):
        weighted[:, head(h)] = gain[:, head(h)] * grad[:, head(h)].astype(F32)


def attend_kernel(parts, chunks, row, q, part, weighted, *rest):
    n = len(parts)
    came, sofar = rest[:n], rest[n:n + 1]
    outs, stats = rest[-2 * n - 1:-1], rest[-1]
    rows, width = q.shape
    keep = in_doc(row, 0)
    first = tag(row, 0)
    square = jnp.zeros((rows, HD), F32)
    inner = jnp.zeros((rows, HD), F32)
    for i, (half, chunk) in enumerate(parts):
        states, attended, carried = came[i], outs[i], outs[n + i]
        size = states.shape[0] - TAG
        same = states[size:size + 1, :] == first
        for h in range(size // HD):
            at = head((half * chunks + chunk) * (size // HD) + h)
            state = jnp.where(same, states[head(h), :], 0.0).astype(BF16)
            carried[head(h), :] = state
            att = (part[:, at] + keep * dot(q[:, at], state, NN)).astype(BF16)
            attended[:, head(h)] = att
            att = att.astype(F32)
            square = square + att * att
            inner = inner + weighted[:, at] * att
    ones = jnp.ones((TAG, HD), F32)
    upper = lax.broadcasted_iota(jnp.int32, (TAG, rows), 0) < TAG // 2
    exact = lax.Precision.HIGHEST
    sums = [
        lax.dot_general(ones, x, (NT, ((), ())), precision=exact, preferred_element_type=F32)
        for x in (square, inner)
    ]
    sums = jnp.where(upper, sums[0], sums[1])
    stats[...] = sums + sofar[0][...] if len(rest) > 3 * n + 1 else sums


def norm_scales(parts):
    feats = HEADS * HD
    total = parts[0][...]
    for x in parts[1:]:
        total = total + x[...]
    inv = lax.rsqrt(total[0:1, :] / feats + 1e-06)
    back = inv * inv * inv * (total[TAG - 1:TAG, :] / feats)
    return as_column(inv), as_column(back)


def grad_kernel(half, chunks, ranks, row, q, weighted, *rest):
    g_out, out = rest[-2:]
    rows, width = g_out.shape
    each = width // HD // chunks
    keep = in_doc(row, 0).astype(BF16)
    inv, back = norm_scales(rest[chunks:chunks + ranks])
    for h in range(width // HD):
        at = head(half * (width // HD) + h)
        att = rest[h // each][:, head(h % each)].astype(F32)
        g = (inv * weighted[:, at] - att * back).astype(BF16)
        g_out[:, head(h)] = g
        out[head(h), :] = dot(q[:, at] * keep, g, TN)
    out[width:, :] = jnp.broadcast_to(tag(row, 0), (TAG, HD))


def back_kernel(chunks, ranks, row, q, scores, gain, k0, k1, v0, v1, g0, g1, *rest):
    attended, carried, rest = rest[:2 * chunks], rest[2 * chunks:4 * chunks], rest[4 * chunks:]
    normed_hbm, grad_q_hbm, part_k, part_v, normed, grad_q, sems = rest[-7:]
    rows, width = k0.shape
    inv, _ = norm_scales(rest[:ranks])
    keep = in_doc(row, 0)
    seen = visible(row)
    n = width // HD
    copies = []
    each = n // chunks
    for half, (k, v, g) in enumerate(((k0, v0, g0), (k1, v1, g1))):
        for h in range(n):
            at = head(half * n + h)
            gh = g[:, head(h)]
            att = attended[half * chunks + h // each][:, head(h % each)].astype(F32)
            state = carried[half * chunks + h // each][head(h % each), :]
            normed[:, at] = (gain[:, at] * att * inv).astype(BF16)
            gs = dot(gh, v[:, head(h)], NT)
            gs = jnp.where(seen, gs, 0.0).astype(BF16)
            whole = dot(gs, k[:, head(h)], NN) + keep * dot(gh, state, NT)
            grad_q[:, at] = whole.astype(BF16)
            part_k[:, at] = dot(gs, q[:, at], TN)
            part_v[:, at] = dot(scores[half * n + h], gh, TN)
        span = slice(half * width, (half + 1) * width)
        for i, (held, out) in enumerate(((normed, normed_hbm), (grad_q, grad_q_hbm))):
            copies.append(
                pltpu.make_async_copy(
                    held.at[:, span], out.at[:, columns(half, width)], sems.at[2 * half + i]
                )
            )
            copies[-1].start()
    for copy in copies:
        copy.wait()


def last_kernel(parts, chunks, row, part_k, part_v, *rest):
    n = len(parts)
    k_hbm, v_hbm, grad_k, grad_v, sems = rest[-5:]
    rows, width = part_k.shape
    keep = in_doc(row, rows - 1)
    last = tag(row, rows - 1)
    copies = []
    for i, (half, chunk) in enumerate(parts):
        states, k, v = rest[3 * i:3 * i + 3]
        size = states.shape[0] - TAG
        same = states[size:size + 1, :] == last
        at_core = core() if half == 0 else 1 - core()
        for h in range(size // HD):
            own = head(chunk * (size // HD) + h)
            at = head((half * chunks + chunk) * (size // HD) + h)
            mine = len(copies) // 2
            later = jnp.where(same, states[head(h), :], 0.0).astype(BF16)
            new_k = part_k[:, at] + keep * dot(v[:, own], later, NT)
            new_v = part_v[:, at] + keep * dot(k[:, own], later, NN)
            grad_k[:, head(mine)] = new_k.astype(BF16)
            grad_v[:, head(mine)] = new_v.astype(BF16)
            start = at_core * (width // 2) + chunk * size + h * HD
            span = pl.ds(pl.multiple_of(start, HD), HD)
            for j, (held, out) in enumerate(((grad_k, k_hbm), (grad_v, v_hbm))):
                copies.append(
                    pltpu.make_async_copy(
                        held.at[:, head(mine)], out.at[:, span], sems.at[2 * mine + j]
                    )
                )
                copies[-1].start()
    for copy in copies:
        copy.wait()


def call(kernel, fixed, outs, args, after=(), scratch=(), aliases={}):
    spaces = [HBM if isinstance(x, list) else VMEM for x in args] + [ANY] * len(after)
    args = [
        pltpu.with_memory_space_constraint(x[0], HBM) if isinstance(x, list) else x for x in args
    ]
    return pl.pallas_call(
        lambda *refs: kernel(*fixed, *refs),
        out_shape=[jax.ShapeDtypeStruct(*out[:2]) for out in outs],
        in_specs=[pl.BlockSpec(memory_space=space) for space in spaces],
        out_specs=[pl.BlockSpec(memory_space=(*out, VMEM)[2]) for out in outs],
        scratch_shapes=scratch,
        input_output_aliases=aliases,
        compiler_params=pltpu.CompilerParams(vmem_limit_bytes=40 * 1024 * 1024),
        name=kernel.__name__[:-7],
    )(*args, *after)


def carry(mine, other, chunks, backward, beside, finish):
    blocks = lax.axis_size("ctx")
    step = -2 if backward else 2

    def swap(value):
        return lax.ppermute(value, "ctx", [(i, i ^ 1) for i in range(blocks)])

    def hop(value):
        return lax.ppermute(value, "ctx", [(i, (i + step) % blocks) for i in range(blocks)])

    sent = other()
    came = swap(sent)
    mine = mine(sent)
    size = (mine.shape[0] - TAG) // chunks
    chunk = ((size + TAG, HD), F32)
    both = call(pair_kernel, [backward], [chunk] * chunks, [mine, came])
    once = [hop(b) for b in both]
    work, token = beside(both[-1])
    window = [call(merge_kernel, [], [chunk], [b, o], [token])[0] for b, o in zip(both, once)]
    entering = [hop(w) for w in window]
    ready = []
    for i, e in enumerate(entering):
        kept, send = call(split_kernel, [backward, i], [chunk] * 2, [e, mine, came])
        ready += [((0, i), kept), ((1, i), swap(send))]
    finish(*map(list, zip(*ready[:-1])), work)
    finish(*map(list, zip(*ready[-1:])), work)
    return work


CHUNKS = 2


def local(queries, key_rows, value_rows, grad_out, doc_ids, out_gain):
    rows, width = queries.shape
    heads = width // HD
    part_width = width // 2
    ranks = lax.axis_size("head")
    ids = doc_ids.reshape(1, rows)
    gain = out_gain.reshape(1, width)
    wide, half, sums = ((rows, width), F32), ((rows, part_width), BF16), ((TAG, rows), F32)
    state = ((part_width + TAG, HD), F32)

    held = {}

    def make_state(which, after=()):
        out, held["k", which], held["v", which], *row = call(
            state_kernel, [which], [state, half, half] + [((1, rows), jnp.int32)] * which,
            [[ids] if which else held["row"], [key_rows], [value_rows]],
            after=after, scratch=[DMA((3,))],
        )
        if which:
            (held["row"],) = row
        return out

    def local_work(token):
        out = call(
            local_kernel, [],
            [((heads, rows, rows), BF16), wide, ((rows, width), BF16), wide, ((1, width), F32)],
            [held["row"], *k, *v, [queries], [grad_out], [gain]],
            after=[token], scratch=[VMEM((rows, width), BF16), DMA((6,))],
        )
        return out, out[1]

    k, v = [], []

    def own_state(sent):
        out = make_state(0, [sent])
        k.extend(held["k", i] for i in range(2))
        v.extend(held["v", i] for i in range(2))
        return out

    attended, carried, stats = {}, {}, []
    piece = part_width // CHUNKS

    def attend(parts, states, work):
        _, part, q, weighted, _ = work
        n = len(parts)
        out = call(
            attend_kernel, [parts, CHUNKS],
            [((rows, piece), BF16)] * n + [((piece, HD), BF16)] * n + [sums],
            [held["row"], q, part, weighted, *states, *stats[-1:]],
        )
        attended.update(zip(parts, out))
        carried.update(zip(parts, out[n:]))
        stats.append(out[-1])

    work = carry(own_state, lambda: make_state(1), CHUNKS, False, local_work, attend)
    scores, part, q, weighted, gain = work
    order = [(which, i) for which in range(2) for i in range(CHUNKS)]
    stats = stats[-1:]
    stats += [
        lax.ppermute(stats[0], "head", [(i, (i + apart) % ranks) for i in range(ranks)])
        for apart in range(1, ranks)
    ]

    def make_grad(which, after=()):
        held["g", which], out = call(
            grad_kernel, [which, CHUNKS, ranks], [half, state],
            [held["row"], q, weighted, *(attended[which, i] for i in range(CHUNKS)), *stats],
            after=after,
        )
        return out

    def back_work(token):
        out = call(
            back_kernel, [CHUNKS, ranks], [((rows, width), BF16, HBM)] * 2 + [wide, wide],
            [held["row"], q, scores, gain, *k, *v, held["g", 0], held["g", 1],
             *(attended[x] for x in order), *(carried[x] for x in order), *stats],
            after=[token],
            scratch=[VMEM((rows, width), BF16), VMEM((rows, width), BF16), DMA((4,))],
        )
        return out, out[2]

    done = []

    def last(parts, states, work):
        args = [held["row"], work[2], work[3]]
        for (which, _), state in zip(parts, states):
            args += [state, k[which], v[which]]
        n = len(args)
        size = len(parts) * piece
        out = call(
            last_kernel, [parts, CHUNKS], [((rows, width), BF16, HBM)] * 2, args,
            after=done[-1] if done else (),
            scratch=[VMEM((rows, size), BF16), VMEM((rows, size), BF16), DMA((2 * size // HD,))],
            aliases={n: 0, n + 1: 1} if done else {},
        )
        done.append(out)

    work = carry(
        lambda sent: make_grad(0, [sent]), lambda: make_grad(1), CHUNKS, True, back_work, last
    )
    return work[0], work[1], *done[-1]


def solution(mesh):
    cut = P("ctx", "head")
    return jax.shard_map(
        local,
        mesh=mesh,
        in_specs=(cut, cut, cut, cut, P("ctx"), P("head")),
        out_specs=(cut, cut, cut, cut),
        check_vma=False,
    )
```

```python
import jax
import jax.numpy as jnp
from jax import lax
from jax.experimental import pallas as pl
from jax.experimental.pallas import tpu as pltpu
from jax.sharding import PartitionSpec as P

HEADS = 32
HD = 128
TAG = 8
F32 = jnp.float32
BF16 = jnp.bfloat16
VMEM, HBM, ANY = pltpu.VMEM, pltpu.HBM, pl.ANY
DMA = pltpu.SemaphoreType.DMA
NN = ((1,), (0,))
NT = ((1,), (1,))
TN = ((0,), (0,))


def dot(a, b, dims):
    return lax.dot_general(a, b, (dims, ((), ())), preferred_element_type=F32)


def head(h):
    return slice(h * HD, (h + 1) * HD)


def core():
    return lax.rem(lax.axis_index("ctx"), 2)


def columns(half, width):
    at = core() if half == 0 else 1 - core()
    return pl.ds(pl.multiple_of(at * width, width), width)


def as_column(row):
    return jnp.transpose(jnp.broadcast_to(row, (HD, row.shape[1])))


def in_doc(row_ref, at):
    row = row_ref[...].astype(F32)
    which = jnp.broadcast_to(row[:, at:at + 1], (row.shape[1], HD))
    return (as_column(row) == which).astype(F32)


def tag(row_ref, at):
    return jnp.broadcast_to(row_ref[:, at:at + 1].astype(F32), (1, HD))


def visible(row_ref):
    rows = row_ref.shape[1]
    row = row_ref[...].astype(F32)
    column = as_column(row)
    column = jnp.concatenate([column] * (rows // HD), axis=1)
    t = lax.broadcasted_iota(jnp.int32, (rows, rows), 0)
    s = lax.broadcasted_iota(jnp.int32, (rows, rows), 1)
    return (column == jnp.broadcast_to(row, (rows, rows))) & (t >= s)


def state_kernel(half, row, k_hbm, v_hbm, *rest):
    if half:
        out, k, v, row_out, sems = rest[-5:]
    else:
        out, k, v, sems = rest[-4:]
    rows, width = k.shape
    span = columns(half, width)
    copies = [
        pltpu.make_async_copy(k_hbm.at[:, span], k, sems.at[1]),
        pltpu.make_async_copy(v_hbm.at[:, span], v, sems.at[2]),
    ]
    if half:
        copies.insert(0, pltpu.make_async_copy(row, row_out, sems.at[0]))
        row = row_out
    for copy in copies:
        copy.start()
    if half:
        copies.pop(0).wait()
    keep = in_doc(row, rows - 1).astype(BF16)
    out[width:, :] = jnp.broadcast_to(tag(row, rows - 1), (TAG, HD))
    for copy in copies:
        copy.wait()
    for h in range(width // HD):
        out[head(h), :] = dot(k[:, head(h)] * keep, v[:, head(h)], TN)


def add_into(out, near, far, near_lo, far_lo):
    size = out.shape[0] - TAG
    near_tag = near[near.shape[0] - TAG:, :]
    same = near_tag[0:1, :] == far[far.shape[0] - TAG:far.shape[0] - TAG + 1, :]
    here = far[far_lo:far_lo + size, :]
    out[:size, :] = near[near_lo:near_lo + size, :] + jnp.where(same, here, 0.0)
    out[size:, :] = near_tag


def pair_kernel(backward, mine, came, *outs):
    size = outs[0].shape[0] - TAG
    upstream = core() == int(backward)

    def fill(down, up):
        for i, out in enumerate(outs):
            add_into(out, down, up, i * size, i * size)

    pl.when(upstream)(lambda: fill(came, mine))
    pl.when(jnp.logical_not(upstream))(lambda: fill(mine, came))


def merge_kernel(near, far, *rest):
    add_into(rest[-1], near, far, 0, 0)


def split_kernel(backward, part, entering, mine, came, *rest):
    keep, send = rest[-2:]
    size = entering.shape[0] - TAG
    upstream = core() == int(backward)

    def fill(to_up, to_down, up):
        to_up[...] = entering[...]
        add_into(to_down, up, entering, part * size, 0)

    pl.when(upstream)(lambda: fill(keep, send, mine))
    pl.when(jnp.logical_not(upstream))(lambda: fill(send, keep, came))


def local_kernel(row, k0, k1, v0, v1, q_hbm, grad_hbm, gain_hbm, *rest):
    scores, part, q, weighted, gain, grad, sems = rest[-7:]
    rows, width = k0.shape
    copies = []
    for i, (hbm, held) in enumerate(((q_hbm, q), (gain_hbm, gain), (grad_hbm, grad))):
        for half in range(2):
            at = slice(half * width, (half + 1) * width)
            copies.append(
                pltpu.make_async_copy(
                    hbm.at[:, columns(half, width)], held.at[:, at], sems.at[2 * i + half]
                )
            )
            copies[-1].start()
    seen = visible(row)
    copies[0].wait()
    copies[1].wait()
    n = width // HD
    for h in range(2 * n):
        k, v = (k0, v0) if h < n else (k1, v1)
        sc = dot(q[:, head(h)], k[:, head(h % n)], NT)
        sc = jnp.where(seen, sc, 0.0).astype(BF16)
        scores[h] = sc
        part[:, head(h)] = dot(sc, v[:, head(h % n)], NN)
    for copy in copies[2:]:
        copy.wait()
    for h in range(2 * n):
        weighted[:, head(h)] = gain[:, head(h)] * grad[:, head(h)].astype(F32)


def attend_kernel(parts, chunks, row, q, part, weighted, *rest):
    n = len(parts)
    came, sofar = rest[:n], rest[n:n + 1]
    outs, stats = rest[-2 * n - 1:-1], rest[-1]
    rows, width = q.shape
    keep = in_doc(row, 0)
    first = tag(row, 0)
    square = jnp.zeros((rows, HD), F32)
    inner = jnp.zeros((rows, HD), F32)
    for i, (half, chunk) in enumerate(parts):
        states, attended, carried = came[i], outs[i], outs[n + i]
        size = states.shape[0] - TAG
        same = states[size:size + 1, :] == first
        for h in range(size // HD):
            at = head((half * chunks + chunk) * (size // HD) + h)
            state = jnp.where(same, states[head(h), :], 0.0).astype(BF16)
            carried[head(h), :] = state
            att = (part[:, at] + keep * dot(q[:, at], state, NN)).astype(BF16)
            attended[:, head(h)] = att
            att = att.astype(F32)
            square = square + att * att
            inner = inner + weighted[:, at] * att
    ones = jnp.ones((TAG, HD), F32)
    upper = lax.broadcasted_iota(jnp.int32, (TAG, rows), 0) < TAG // 2
    exact = lax.Precision.HIGHEST
    sums = [
        lax.dot_general(ones, x, (NT, ((), ())), precision=exact, preferred_element_type=F32)
        for x in (square, inner)
    ]
    sums = jnp.where(upper, sums[0], sums[1])
    stats[...] = sums + sofar[0][...] if len(rest) > 3 * n + 1 else sums


def norm_scales(parts):
    feats = HEADS * HD
    total = parts[0][...]
    for x in parts[1:]:
        total = total + x[...]
    inv = lax.rsqrt(total[0:1, :] / feats + 1e-06)
    back = inv * inv * inv * (total[TAG - 1:TAG, :] / feats)
    return as_column(inv), as_column(back)


def grad_kernel(half, chunks, ranks, row, q, weighted, *rest):
    g_out, out = rest[-2:]
    rows, width = g_out.shape
    each = width // HD // chunks
    keep = in_doc(row, 0).astype(BF16)
    inv, back = norm_scales(rest[chunks:chunks + ranks])
    for h in range(width // HD):
        at = head(half * (width // HD) + h)
        att = rest[h // each][:, head(h % each)].astype(F32)
        g = (inv * weighted[:, at] - att * back).astype(BF16)
        g_out[:, head(h)] = g
        out[head(h), :] = dot(q[:, at] * keep, g, TN)
    out[width:, :] = jnp.broadcast_to(tag(row, 0), (TAG, HD))


def back_kernel(chunks, ranks, row, q, scores, gain, k0, k1, v0, v1, g0, g1, *rest):
    attended, carried, rest = rest[:2 * chunks], rest[2 * chunks:4 * chunks], rest[4 * chunks:]
    normed_hbm, grad_q_hbm, part_k, part_v, normed, grad_q, sems = rest[-7:]
    rows, width = k0.shape
    inv, _ = norm_scales(rest[:ranks])
    keep = in_doc(row, 0)
    seen = visible(row)
    n = width // HD
    copies = []
    each = n // chunks
    for half, (k, v, g) in enumerate(((k0, v0, g0), (k1, v1, g1))):
        for h in range(n):
            at = head(half * n + h)
            gh = g[:, head(h)]
            att = attended[half * chunks + h // each][:, head(h % each)].astype(F32)
            state = carried[half * chunks + h // each][head(h % each), :]
            normed[:, at] = (gain[:, at] * att * inv).astype(BF16)
            gs = dot(gh, v[:, head(h)], NT)
            gs = jnp.where(seen, gs, 0.0).astype(BF16)
            whole = dot(gs, k[:, head(h)], NN) + keep * dot(gh, state, NT)
            grad_q[:, at] = whole.astype(BF16)
            part_k[:, at] = dot(gs, q[:, at], TN)
            part_v[:, at] = dot(scores[half * n + h], gh, TN)
        span = slice(half * width, (half + 1) * width)
        for i, (held, out) in enumerate(((normed, normed_hbm), (grad_q, grad_q_hbm))):
            copies.append(
                pltpu.make_async_copy(
                    held.at[:, span], out.at[:, columns(half, width)], sems.at[2 * half + i]
                )
            )
            copies[-1].start()
    for copy in copies:
        copy.wait()


def last_kernel(parts, chunks, row, part_k, part_v, *rest):
    n = len(parts)
    k_hbm, v_hbm, grad_k, grad_v, sems = rest[-5:]
    rows, width = part_k.shape
    keep = in_doc(row, rows - 1)
    last = tag(row, rows - 1)
    copies = []
    for i, (half, chunk) in enumerate(parts):
        states, k, v = rest[3 * i:3 * i + 3]
        size = states.shape[0] - TAG
        same = states[size:size + 1, :] == last
        at_core = core() if half == 0 else 1 - core()
        for h in range(size // HD):
            own = head(chunk * (size // HD) + h)
            at = head((half * chunks + chunk) * (size // HD) + h)
            mine = len(copies) // 2
            later = jnp.where(same, states[head(h), :], 0.0).astype(BF16)
            new_k = part_k[:, at] + keep * dot(v[:, own], later, NT)
            new_v = part_v[:, at] + keep * dot(k[:, own], later, NN)
            grad_k[:, head(mine)] = new_k.astype(BF16)
            grad_v[:, head(mine)] = new_v.astype(BF16)
            start = at_core * (width // 2) + chunk * size + h * HD
            span = pl.ds(pl.multiple_of(start, HD), HD)
            for j, (held, out) in enumerate(((grad_k, k_hbm), (grad_v, v_hbm))):
                copies.append(
                    pltpu.make_async_copy(
                        held.at[:, head(mine)], out.at[:, span], sems.at[2 * mine + j]
                    )
                )
                copies[-1].start()
    for copy in copies:
        copy.wait()


def call(kernel, fixed, outs, args, after=(), scratch=(), aliases={}):
    spaces = [HBM if isinstance(x, list) else VMEM for x in args] + [ANY] * len(after)
    args = [
        pltpu.with_memory_space_constraint(x[0], HBM) if isinstance(x, list) else x for x in args
    ]
    return pl.pallas_call(
        lambda *refs: kernel(*fixed, *refs),
        out_shape=[jax.ShapeDtypeStruct(*out[:2]) for out in outs],
        in_specs=[pl.BlockSpec(memory_space=space) for space in spaces],
        out_specs=[pl.BlockSpec(memory_space=(*out, VMEM)[2]) for out in outs],
        scratch_shapes=scratch,
        input_output_aliases=aliases,
        compiler_params=pltpu.CompilerParams(vmem_limit_bytes=40 * 1024 * 1024),
        name=kernel.__name__[:-7],
    )(*args, *after)


def carry(mine, other, chunks, backward, beside, finish):
    blocks = lax.axis_size("ctx")
    step = -2 if backward else 2

    def swap(value):
        return lax.ppermute(value, "ctx", [(i, i ^ 1) for i in range(blocks)])

    def hop(value):
        return lax.ppermute(value, "ctx", [(i, (i + step) % blocks) for i in range(blocks)])

    sent = other()
    came = swap(sent)
    mine = mine(sent)
    size = (mine.shape[0] - TAG) // chunks
    chunk = ((size + TAG, HD), F32)
    both = call(pair_kernel, [backward], [chunk] * chunks, [mine, came])
    once = [hop(b) for b in both]
    work, token = beside(both[-1])
    window = [call(merge_kernel, [], [chunk], [b, o], [token])[0] for b, o in zip(both, once)]
    entering = [hop(w) for w in window]
    ready = []
    for i, e in enumerate(entering):
        kept, send = call(split_kernel, [backward, i], [chunk] * 2, [e, mine, came])
        ready += [((0, i), kept), ((1, i), swap(send))]
    finish(*map(list, zip(*ready[:-1])), work)
    finish(*map(list, zip(*ready[-1:])), work)
    return work


CHUNKS = 4


def local(queries, key_rows, value_rows, grad_out, doc_ids, out_gain):
    rows, width = queries.shape
    heads = width // HD
    part_width = width // 2
    ranks = lax.axis_size("head")
    ids = doc_ids.reshape(1, rows)
    gain = out_gain.reshape(1, width)
    wide, half, sums = ((rows, width), F32), ((rows, part_width), BF16), ((TAG, rows), F32)
    state = ((part_width + TAG, HD), F32)

    held = {}

    def make_state(which, after=()):
        out, held["k", which], held["v", which], *row = call(
            state_kernel, [which], [state, half, half] + [((1, rows), jnp.int32)] * which,
            [[ids] if which else held["row"], [key_rows], [value_rows]],
            after=after, scratch=[DMA((3,))],
        )
        if which:
            (held["row"],) = row
        return out

    def local_work(token):
        out = call(
            local_kernel, [],
            [((heads, rows, rows), BF16), wide, ((rows, width), BF16), wide, ((1, width), F32)],
            [held["row"], *k, *v, [queries], [grad_out], [gain]],
            after=[token], scratch=[VMEM((rows, width), BF16), DMA((6,))],
        )
        return out, out[1]

    k, v = [], []

    def own_state(sent):
        out = make_state(0, [sent])
        k.extend(held["k", i] for i in range(2))
        v.extend(held["v", i] for i in range(2))
        return out

    attended, carried, stats = {}, {}, []
    piece = part_width // CHUNKS

    def attend(parts, states, work):
        _, part, q, weighted, _ = work
        n = len(parts)
        out = call(
            attend_kernel, [parts, CHUNKS],
            [((rows, piece), BF16)] * n + [((piece, HD), BF16)] * n + [sums],
            [held["row"], q, part, weighted, *states, *stats[-1:]],
        )
        attended.update(zip(parts, out))
        carried.update(zip(parts, out[n:]))
        stats.append(out[-1])

    work = carry(own_state, lambda: make_state(1), CHUNKS, False, local_work, attend)
    scores, part, q, weighted, gain = work
    order = [(which, i) for which in range(2) for i in range(CHUNKS)]
    stats = stats[-1:]
    stats += [
        lax.ppermute(stats[0], "head", [(i, (i + apart) % ranks) for i in range(ranks)])
        for apart in range(1, ranks)
    ]

    def make_grad(which, after=()):
        held["g", which], out = call(
            grad_kernel, [which, CHUNKS, ranks], [half, state],
            [held["row"], q, weighted, *(attended[which, i] for i in range(CHUNKS)), *stats],
            after=after,
        )
        return out

    def back_work(token):
        out = call(
            back_kernel, [CHUNKS, ranks], [((rows, width), BF16, HBM)] * 2 + [wide, wide],
            [held["row"], q, scores, gain, *k, *v, held["g", 0], held["g", 1],
             *(attended[x] for x in order), *(carried[x] for x in order), *stats],
            after=[token],
            scratch=[VMEM((rows, width), BF16), VMEM((rows, width), BF16), DMA((4,))],
        )
        return out, out[2]

    done = []

    def last(parts, states, work):
        args = [held["row"], work[2], work[3]]
        for (which, _), state in zip(parts, states):
            args += [state, k[which], v[which]]
        n = len(args)
        size = len(parts) * piece
        out = call(
            last_kernel, [parts, CHUNKS], [((rows, width), BF16, HBM)] * 2, args,
            after=done[-1] if done else (),
            scratch=[VMEM((rows, size), BF16), VMEM((rows, size), BF16), DMA((2 * size // HD,))],
            aliases={n: 0, n + 1: 1} if done else {},
        )
        done.append(out)

    work = carry(
        lambda sent: make_grad(0, [sent]), lambda: make_grad(1), CHUNKS, True, back_work, last
    )
    return work[0], work[1], *done[-1]


def solution(mesh):
    cut = P("ctx", "head")
    return jax.shard_map(
        local,
        mesh=mesh,
        in_specs=(cut, cut, cut, cut, P("ctx"), P("head")),
        out_specs=(cut, cut, cut, cut),
        check_vma=False,
    )
```

```python
import jax
import jax.numpy as jnp
from jax import lax
from jax.experimental import pallas as pl
from jax.experimental.pallas import tpu as pltpu
from jax.sharding import PartitionSpec as P

HEADS = 32
HD = 128
TAG = 8
F32 = jnp.float32
BF16 = jnp.bfloat16
VMEM, HBM, ANY = pltpu.VMEM, pltpu.HBM, pl.ANY
DMA = pltpu.SemaphoreType.DMA
NN = ((1,), (0,))
NT = ((1,), (1,))
TN = ((0,), (0,))


def dot(a, b, dims):
    return lax.dot_general(a, b, (dims, ((), ())), preferred_element_type=F32)


def head(h):
    return slice(h * HD, (h + 1) * HD)


def core():
    return lax.rem(lax.axis_index("ctx"), 2)


def columns(half, width):
    at = core() if half == 0 else 1 - core()
    return pl.ds(pl.multiple_of(at * width, width), width)


def as_column(row):
    return jnp.transpose(jnp.broadcast_to(row, (HD, row.shape[1])))


def in_doc(row_ref, at):
    row = row_ref[...].astype(F32)
    which = jnp.broadcast_to(row[:, at:at + 1], (row.shape[1], HD))
    return (as_column(row) == which).astype(F32)


def tag(row_ref, at):
    return jnp.broadcast_to(row_ref[:, at:at + 1].astype(F32), (1, HD))


def visible(row_ref):
    rows = row_ref.shape[1]
    row = row_ref[...].astype(F32)
    column = as_column(row)
    column = jnp.concatenate([column] * (rows // HD), axis=1)
    t = lax.broadcasted_iota(jnp.int32, (rows, rows), 0)
    s = lax.broadcasted_iota(jnp.int32, (rows, rows), 1)
    return (column == jnp.broadcast_to(row, (rows, rows))) & (t >= s)


def state_kernel(half, row, k_hbm, v_hbm, *rest):
    if half:
        out, k, v, row_out, sems = rest[-5:]
    else:
        out, k, v, sems = rest[-4:]
    rows, width = k.shape
    span = columns(half, width)
    copies = [
        pltpu.make_async_copy(k_hbm.at[:, span], k, sems.at[1]),
        pltpu.make_async_copy(v_hbm.at[:, span], v, sems.at[2]),
    ]
    if half:
        copies.insert(0, pltpu.make_async_copy(row, row_out, sems.at[0]))
        row = row_out
    for copy in copies:
        copy.start()
    if half:
        copies.pop(0).wait()
    keep = in_doc(row, rows - 1).astype(BF16)
    out[width:, :] = jnp.broadcast_to(tag(row, rows - 1), (TAG, HD))
    for copy in copies:
        copy.wait()
    for h in range(width // HD):
        out[head(h), :] = dot(k[:, head(h)] * keep, v[:, head(h)], TN)


def add_into(out, near, far, near_lo, far_lo):
    size = out.shape[0] - TAG
    near_tag = near[near.shape[0] - TAG:, :]
    same = near_tag[0:1, :] == far[far.shape[0] - TAG:far.shape[0] - TAG + 1, :]
    here = far[far_lo:far_lo + size, :]
    out[:size, :] = near[near_lo:near_lo + size, :] + jnp.where(same, here, 0.0)
    out[size:, :] = near_tag


def pair_kernel(backward, mine, came, *outs):
    size = outs[0].shape[0] - TAG
    upstream = core() == int(backward)

    def fill(down, up):
        for i, out in enumerate(outs):
            add_into(out, down, up, i * size, i * size)

    pl.when(upstream)(lambda: fill(came, mine))
    pl.when(jnp.logical_not(upstream))(lambda: fill(mine, came))


def merge_kernel(near, far, *rest):
    add_into(rest[-1], near, far, 0, 0)


def split_kernel(backward, part, entering, mine, came, *rest):
    keep, send = rest[-2:]
    size = entering.shape[0] - TAG
    upstream = core() == int(backward)

    def fill(to_up, to_down, up):
        to_up[...] = entering[...]
        add_into(to_down, up, entering, part * size, 0)

    pl.when(upstream)(lambda: fill(keep, send, mine))
    pl.when(jnp.logical_not(upstream))(lambda: fill(send, keep, came))


def local_kernel(row, k0, k1, v0, v1, q_hbm, grad_hbm, gain_hbm, *rest):
    scores, part, q, weighted, gain, grad, sems = rest[-7:]
    rows, width = k0.shape
    copies = []
    for i, (hbm, held) in enumerate(((q_hbm, q), (gain_hbm, gain), (grad_hbm, grad))):
        for half in range(2):
            at = slice(half * width, (half + 1) * width)
            copies.append(
                pltpu.make_async_copy(
                    hbm.at[:, columns(half, width)], held.at[:, at], sems.at[2 * i + half]
                )
            )
            copies[-1].start()
    seen = visible(row)
    copies[0].wait()
    copies[1].wait()
    n = width // HD
    for h in range(2 * n):
        k, v = (k0, v0) if h < n else (k1, v1)
        sc = dot(q[:, head(h)], k[:, head(h % n)], NT)
        sc = jnp.where(seen, sc, 0.0).astype(BF16)
        scores[h] = sc
        part[:, head(h)] = dot(sc, v[:, head(h % n)], NN)
    for copy in copies[2:]:
        copy.wait()
    for h in range(2 * n):
        weighted[:, head(h)] = gain[:, head(h)] * grad[:, head(h)].astype(F32)


def attend_kernel(parts, chunks, row, q, part, weighted, *rest):
    n = len(parts)
    came, sofar = rest[:n], rest[n:n + 1]
    outs, stats = rest[-2 * n - 1:-1], rest[-1]
    rows, width = q.shape
    keep = in_doc(row, 0)
    first = tag(row, 0)
    square = jnp.zeros((rows, HD), F32)
    inner = jnp.zeros((rows, HD), F32)
    for i, (half, chunk) in enumerate(parts):
        states, attended, carried = came[i], outs[i], outs[n + i]
        size = states.shape[0] - TAG
        same = states[size:size + 1, :] == first
        for h in range(size // HD):
            at = head((half * chunks + chunk) * (size // HD) + h)
            state = jnp.where(same, states[head(h), :], 0.0).astype(BF16)
            carried[head(h), :] = state
            att = (part[:, at] + keep * dot(q[:, at], state, NN)).astype(BF16)
            attended[:, head(h)] = att
            att = att.astype(F32)
            square = square + att * att
            inner = inner + weighted[:, at] * att
    ones = jnp.ones((TAG, HD), F32)
    upper = lax.broadcasted_iota(jnp.int32, (TAG, rows), 0) < TAG // 2
    exact = lax.Precision.HIGHEST
    sums = [
        lax.dot_general(ones, x, (NT, ((), ())), precision=exact, preferred_element_type=F32)
        for x in (square, inner)
    ]
    sums = jnp.where(upper, sums[0], sums[1])
    stats[...] = sums + sofar[0][...] if len(rest) > 3 * n + 1 else sums


def norm_scales(parts):
    feats = HEADS * HD
    total = parts[0][...]
    for x in parts[1:]:
        total = total + x[...]
    inv = lax.rsqrt(total[0:1, :] / feats + 1e-06)
    back = inv * inv * inv * (total[TAG - 1:TAG, :] / feats)
    return as_column(inv), as_column(back)


def grad_kernel(half, chunks, ranks, row, q, weighted, *rest):
    g_out, out = rest[-2:]
    rows, width = g_out.shape
    each = width // HD // chunks
    keep = in_doc(row, 0).astype(BF16)
    inv, back = norm_scales(rest[chunks:chunks + ranks])
    for h in range(width // HD):
        at = head(half * (width // HD) + h)
        att = rest[h // each][:, head(h % each)].astype(F32)
        g = (inv * weighted[:, at] - att * back).astype(BF16)
        g_out[:, head(h)] = g
        out[head(h), :] = dot(q[:, at] * keep, g, TN)
    out[width:, :] = jnp.broadcast_to(tag(row, 0), (TAG, HD))


def back_kernel(chunks, ranks, row, q, scores, gain, k0, k1, v0, v1, g0, g1, *rest):
    attended, carried, rest = rest[:2 * chunks], rest[2 * chunks:4 * chunks], rest[4 * chunks:]
    normed_hbm, grad_q_hbm, part_k, part_v, normed, grad_q, sems = rest[-7:]
    rows, width = k0.shape
    inv, _ = norm_scales(rest[:ranks])
    keep = in_doc(row, 0)
    seen = visible(row)
    n = width // HD
    copies = []
    each = n // chunks
    for half, (k, v, g) in enumerate(((k0, v0, g0), (k1, v1, g1))):
        for h in range(n):
            at = head(half * n + h)
            gh = g[:, head(h)]
            att = attended[half * chunks + h // each][:, head(h % each)].astype(F32)
            state = carried[half * chunks + h // each][head(h % each), :]
            normed[:, at] = (gain[:, at] * att * inv).astype(BF16)
            gs = dot(gh, v[:, head(h)], NT)
            gs = jnp.where(seen, gs, 0.0).astype(BF16)
            whole = dot(gs, k[:, head(h)], NN) + keep * dot(gh, state, NT)
            grad_q[:, at] = whole.astype(BF16)
            part_k[:, at] = dot(gs, q[:, at], TN)
            part_v[:, at] = dot(scores[half * n + h], gh, TN)
        span = slice(half * width, (half + 1) * width)
        for i, (held, out) in enumerate(((normed, normed_hbm), (grad_q, grad_q_hbm))):
            copies.append(
                pltpu.make_async_copy(
                    held.at[:, span], out.at[:, columns(half, width)], sems.at[2 * half + i]
                )
            )
            copies[-1].start()
    for copy in copies:
        copy.wait()


def last_kernel(parts, chunks, row, part_k, part_v, *rest):
    n = len(parts)
    k_hbm, v_hbm, grad_k, grad_v, sems = rest[-5:]
    rows, width = part_k.shape
    keep = in_doc(row, rows - 1)
    last = tag(row, rows - 1)
    copies = []
    for i, (half, chunk) in enumerate(parts):
        states, k, v = rest[3 * i:3 * i + 3]
        size = states.shape[0] - TAG
        same = states[size:size + 1, :] == last
        at_core = core() if half == 0 else 1 - core()
        for h in range(size // HD):
            own = head(chunk * (size // HD) + h)
            at = head((half * chunks + chunk) * (size // HD) + h)
            mine = len(copies) // 2
            later = jnp.where(same, states[head(h), :], 0.0).astype(BF16)
            new_k = part_k[:, at] + keep * dot(v[:, own], later, NT)
            new_v = part_v[:, at] + keep * dot(k[:, own], later, NN)
            grad_k[:, head(mine)] = new_k.astype(BF16)
            grad_v[:, head(mine)] = new_v.astype(BF16)
            start = at_core * (width // 2) + chunk * size + h * HD
            span = pl.ds(pl.multiple_of(start, HD), HD)
            for j, (held, out) in enumerate(((grad_k, k_hbm), (grad_v, v_hbm))):
                copies.append(
                    pltpu.make_async_copy(
                        held.at[:, head(mine)], out.at[:, span], sems.at[2 * mine + j]
                    )
                )
                copies[-1].start()
    for copy in copies:
        copy.wait()


def call(kernel, fixed, outs, args, after=(), scratch=(), aliases={}):
    spaces = [HBM if isinstance(x, list) else VMEM for x in args] + [ANY] * len(after)
    args = [
        pltpu.with_memory_space_constraint(x[0], HBM) if isinstance(x, list) else x for x in args
    ]
    return pl.pallas_call(
        lambda *refs: kernel(*fixed, *refs),
        out_shape=[jax.ShapeDtypeStruct(*out[:2]) for out in outs],
        in_specs=[pl.BlockSpec(memory_space=space) for space in spaces],
        out_specs=[pl.BlockSpec(memory_space=(*out, VMEM)[2]) for out in outs],
        scratch_shapes=scratch,
        input_output_aliases=aliases,
        compiler_params=pltpu.CompilerParams(vmem_limit_bytes=40 * 1024 * 1024),
        name=kernel.__name__[:-7],
    )(*args, *after)


def carry(mine, other, chunks, backward, beside, finish):
    blocks = lax.axis_size("ctx")
    step = -2 if backward else 2

    def swap(value):
        return lax.ppermute(value, "ctx", [(i, i ^ 1) for i in range(blocks)])

    def hop(value):
        return lax.ppermute(value, "ctx", [(i, (i + step) % blocks) for i in range(blocks)])

    sent = other()
    came = swap(sent)
    mine = mine(sent)
    size = (mine.shape[0] - TAG) // chunks
    chunk = ((size + TAG, HD), F32)
    both = call(pair_kernel, [backward], [chunk] * chunks, [mine, came])
    once = [hop(b) for b in both]
    work, token = beside(both[-1])
    window = [call(merge_kernel, [], [chunk], [b, o], [token])[0] for b, o in zip(both, once)]
    entering = [hop(w) for w in window]
    ready = []
    for i, e in enumerate(entering):
        kept, send = call(split_kernel, [backward, i], [chunk] * 2, [e, mine, came])
        ready += [((0, i), kept), ((1, i), swap(send))]
    finish(*map(list, zip(*ready[:-1])), work)
    finish(*map(list, zip(*ready[-1:])), work)
    return work


CHUNKS = 2


def local(queries, key_rows, value_rows, grad_out, doc_ids, out_gain):
    rows, width = queries.shape
    heads = width // HD
    part_width = width // 2
    ranks = lax.axis_size("head")
    blocks = lax.axis_size("ctx")
    ids = doc_ids.reshape(1, rows)
    gain = out_gain.reshape(1, width)
    wide, half, sums = ((rows, width), F32), ((rows, part_width), BF16), ((TAG, rows), F32)
    state = ((part_width + TAG, HD), F32)

    held = {}

    def make_state(which, after=()):
        out, held["k", which], held["v", which], *row = call(
            state_kernel, [which], [state, half, half] + [((1, rows), jnp.int32)] * which,
            [[ids] if which else held["row"], [key_rows], [value_rows]],
            after=after, scratch=[DMA((3,))],
        )
        if which:
            (held["row"],) = row
        return out

    def local_work(token):
        out = call(
            local_kernel, [],
            [((heads, rows, rows), BF16), wide, ((rows, width), BF16), wide, ((1, width), F32)],
            [held["row"], *k, *v, [queries], [grad_out], [gain]],
            after=[token], scratch=[VMEM((rows, width), BF16), DMA((6,))],
        )
        return out, out[1]

    k, v = [], []

    def own_state(sent):
        out = make_state(0, [sent])
        k.extend(held["k", i] for i in range(2))
        v.extend(held["v", i] for i in range(2))
        return out

    attended, carried, stats = {}, {}, []
    piece = part_width // CHUNKS

    def attend(parts, states, work):
        _, part, q, weighted, _ = work
        n = len(parts)
        out = call(
            attend_kernel, [parts, CHUNKS],
            [((rows, piece), BF16)] * n + [((piece, HD), BF16)] * n + [sums],
            [held["row"], q, part, weighted, *states, *stats[-1:]],
        )
        attended.update(zip(parts, out))
        carried.update(zip(parts, out[n:]))
        stats.append(out[-1])

    work = carry(own_state, lambda: make_state(1), CHUNKS, False, local_work, attend)
    scores, part, q, weighted, gain = work
    order = [(which, i) for which in range(2) for i in range(CHUNKS)]
    stats = stats[-1:]

    def around(apart):
        return [
            (c * ranks + i, c * ranks + (i + (apart if c % 2 else -apart)) % ranks)
            for c in range(blocks) for i in range(ranks)
        ]

    stats += [
        lax.ppermute(stats[0], ("ctx", "head"), around(apart)) for apart in range(1, ranks)
    ]

    def make_grad(which, after=()):
        held["g", which], out = call(
            grad_kernel, [which, CHUNKS, ranks], [half, state],
            [held["row"], q, weighted, *(attended[which, i] for i in range(CHUNKS)), *stats],
            after=after,
        )
        return out

    def back_work(token):
        out = call(
            back_kernel, [CHUNKS, ranks], [((rows, width), BF16, HBM)] * 2 + [wide, wide],
            [held["row"], q, scores, gain, *k, *v, held["g", 0], held["g", 1],
             *(attended[x] for x in order), *(carried[x] for x in order), *stats],
            after=[token],
            scratch=[VMEM((rows, width), BF16), VMEM((rows, width), BF16), DMA((4,))],
        )
        return out, out[2]

    done = []

    def last(parts, states, work):
        args = [held["row"], work[2], work[3]]
        for (which, _), state in zip(parts, states):
            args += [state, k[which], v[which]]
        n = len(args)
        size = len(parts) * piece
        out = call(
            last_kernel, [parts, CHUNKS], [((rows, width), BF16, HBM)] * 2, args,
            after=done[-1] if done else (),
            scratch=[VMEM((rows, size), BF16), VMEM((rows, size), BF16), DMA((2 * size // HD,))],
            aliases={n: 0, n + 1: 1} if done else {},
        )
        done.append(out)

    work = carry(
        lambda sent: make_grad(0, [sent]), lambda: make_grad(1), CHUNKS, True, back_work, last
    )
    return work[0], work[1], *done[-1]


def solution(mesh):
    cut = P("ctx", "head")
    return jax.shard_map(
        local,
        mesh=mesh,
        in_specs=(cut, cut, cut, cut, P("ctx"), P("head")),
        out_specs=(cut, cut, cut, cut),
        check_vma=False,
    )
```

```python
import jax
import jax.numpy as jnp
from jax import lax
from jax.experimental import pallas as pl
from jax.experimental.pallas import tpu as pltpu
from jax.sharding import PartitionSpec as P

HEADS = 32
HD = 128
TAG = 8
F32 = jnp.float32
BF16 = jnp.bfloat16
VMEM, HBM, ANY = pltpu.VMEM, pltpu.HBM, pl.ANY
DMA = pltpu.SemaphoreType.DMA
NN = ((1,), (0,))
NT = ((1,), (1,))
TN = ((0,), (0,))


def dot(a, b, dims):
    return lax.dot_general(a, b, (dims, ((), ())), preferred_element_type=F32)


def head(h):
    return slice(h * HD, (h + 1) * HD)


def core():
    return lax.rem(lax.axis_index("ctx"), 2)


def columns(half, width):
    at = core() if half == 0 else 1 - core()
    return pl.ds(pl.multiple_of(at * width, width), width)


def as_column(row):
    return jnp.transpose(jnp.broadcast_to(row, (HD, row.shape[1])))


def in_doc(row_ref, at):
    row = row_ref[...].astype(F32)
    which = jnp.broadcast_to(row[:, at:at + 1], (row.shape[1], HD))
    return (as_column(row) == which).astype(F32)


def tag(row_ref, at):
    return jnp.broadcast_to(row_ref[:, at:at + 1].astype(F32), (1, HD))


def visible(row_ref):
    rows = row_ref.shape[1]
    row = row_ref[...].astype(F32)
    column = as_column(row)
    column = jnp.concatenate([column] * (rows // HD), axis=1)
    t = lax.broadcasted_iota(jnp.int32, (rows, rows), 0)
    s = lax.broadcasted_iota(jnp.int32, (rows, rows), 1)
    return (column == jnp.broadcast_to(row, (rows, rows))) & (t >= s)


def state_kernel(half, row, k_hbm, v_hbm, *rest):
    if half:
        out, k, v, row_out, sems = rest[-5:]
    else:
        out, k, v, sems = rest[-4:]
    rows, width = k.shape
    span = columns(half, width)
    copies = [
        pltpu.make_async_copy(k_hbm.at[:, span], k, sems.at[1]),
        pltpu.make_async_copy(v_hbm.at[:, span], v, sems.at[2]),
    ]
    if half:
        copies.insert(0, pltpu.make_async_copy(row, row_out, sems.at[0]))
        row = row_out
    for copy in copies:
        copy.start()
    if half:
        copies.pop(0).wait()
    keep = in_doc(row, rows - 1).astype(BF16)
    out[width:, :] = jnp.broadcast_to(tag(row, rows - 1), (TAG, HD))
    for copy in copies:
        copy.wait()
    for h in range(width // HD):
        out[head(h), :] = dot(k[:, head(h)] * keep, v[:, head(h)], TN)


def add_into(out, near, far, near_lo, far_lo):
    size = out.shape[0] - TAG
    near_tag = near[near.shape[0] - TAG:, :]
    same = near_tag[0:1, :] == far[far.shape[0] - TAG:far.shape[0] - TAG + 1, :]
    here = far[far_lo:far_lo + size, :]
    out[:size, :] = near[near_lo:near_lo + size, :] + jnp.where(same, here, 0.0)
    out[size:, :] = near_tag


def pair_kernel(backward, mine, came, *outs):
    size = outs[0].shape[0] - TAG
    upstream = core() == int(backward)

    def fill(down, up):
        for i, out in enumerate(outs):
            add_into(out, down, up, i * size, i * size)

    pl.when(upstream)(lambda: fill(came, mine))
    pl.when(jnp.logical_not(upstream))(lambda: fill(mine, came))


def merge_kernel(near, far, *rest):
    add_into(rest[-1], near, far, 0, 0)


def split_kernel(backward, part, entering, mine, came, *rest):
    keep, send = rest[-2:]
    size = entering.shape[0] - TAG
    upstream = core() == int(backward)

    def fill(to_up, to_down, up):
        to_up[...] = entering[...]
        add_into(to_down, up, entering, part * size, 0)

    pl.when(upstream)(lambda: fill(keep, send, mine))
    pl.when(jnp.logical_not(upstream))(lambda: fill(send, keep, came))


def local_kernel(row, k0, k1, v0, v1, q_hbm, grad_hbm, gain_hbm, *rest):
    scores, part, q, weighted, gain, grad, sems = rest[-7:]
    rows, width = k0.shape
    copies = []
    for i, (hbm, held) in enumerate(((q_hbm, q), (gain_hbm, gain), (grad_hbm, grad))):
        for half in range(2):
            at = slice(half * width, (half + 1) * width)
            copies.append(
                pltpu.make_async_copy(
                    hbm.at[:, columns(half, width)], held.at[:, at], sems.at[2 * i + half]
                )
            )
            copies[-1].start()
    seen = visible(row)
    copies[0].wait()
    copies[1].wait()
    n = width // HD
    for h in range(2 * n):
        k, v = (k0, v0) if h < n else (k1, v1)
        sc = dot(q[:, head(h)], k[:, head(h % n)], NT)
        sc = jnp.where(seen, sc, 0.0).astype(BF16)
        scores[h] = sc
        part[:, head(h)] = dot(sc, v[:, head(h % n)], NN)
    for copy in copies[2:]:
        copy.wait()
    for h in range(2 * n):
        weighted[:, head(h)] = gain[:, head(h)] * grad[:, head(h)].astype(F32)


def attend_kernel(parts, chunks, row, q, part, weighted, *rest):
    n = len(parts)
    came, sofar = rest[:n], rest[n:n + 1]
    outs, stats = rest[-2 * n - 1:-1], rest[-1]
    rows, width = q.shape
    keep = in_doc(row, 0)
    first = tag(row, 0)
    square = jnp.zeros((rows, HD), F32)
    inner = jnp.zeros((rows, HD), F32)
    for i, (half, chunk) in enumerate(parts):
        states, attended, carried = came[i], outs[i], outs[n + i]
        size = states.shape[0] - TAG
        same = states[size:size + 1, :] == first
        for h in range(size // HD):
            at = head((half * chunks + chunk) * (size // HD) + h)
            state = jnp.where(same, states[head(h), :], 0.0).astype(BF16)
            carried[head(h), :] = state
            att = (part[:, at] + keep * dot(q[:, at], state, NN)).astype(BF16)
            attended[:, head(h)] = att
            att = att.astype(F32)
            square = square + att * att
            inner = inner + weighted[:, at] * att
    ones = jnp.ones((TAG, HD), F32)
    upper = lax.broadcasted_iota(jnp.int32, (TAG, rows), 0) < TAG // 2
    exact = lax.Precision.HIGHEST
    sums = [
        lax.dot_general(ones, x, (NT, ((), ())), precision=exact, preferred_element_type=F32)
        for x in (square, inner)
    ]
    sums = jnp.where(upper, sums[0], sums[1])
    stats[...] = sums + sofar[0][...] if len(rest) > 3 * n + 1 else sums


def norm_scales(parts):
    feats = HEADS * HD
    total = parts[0][...]
    for x in parts[1:]:
        total = total + x[...]
    inv = lax.rsqrt(total[0:1, :] / feats + 1e-06)
    back = inv * inv * inv * (total[TAG - 1:TAG, :] / feats)
    return as_column(inv), as_column(back)


def grad_kernel(half, chunks, ranks, row, q, weighted, *rest):
    g_out, out = rest[-2:]
    rows, width = g_out.shape
    each = width // HD // chunks
    keep = in_doc(row, 0).astype(BF16)
    inv, back = norm_scales(rest[chunks:chunks + ranks])
    for h in range(width // HD):
        at = head(half * (width // HD) + h)
        att = rest[h // each][:, head(h % each)].astype(F32)
        g = (inv * weighted[:, at] - att * back).astype(BF16)
        g_out[:, head(h)] = g
        out[head(h), :] = dot(q[:, at] * keep, g, TN)
    out[width:, :] = jnp.broadcast_to(tag(row, 0), (TAG, HD))


def back_kernel(chunks, ranks, row, q, scores, gain, k0, k1, v0, v1, g0, g1, *rest):
    attended, carried, rest = rest[:2 * chunks], rest[2 * chunks:4 * chunks], rest[4 * chunks:]
    normed_hbm, grad_q_hbm, part_k, part_v, normed, grad_q, sems = rest[-7:]
    rows, width = k0.shape
    inv, _ = norm_scales(rest[:ranks])
    keep = in_doc(row, 0)
    seen = visible(row)
    n = width // HD
    copies = []
    each = n // chunks
    for half, (k, v, g) in enumerate(((k0, v0, g0), (k1, v1, g1))):
        for h in range(n):
            at = head(half * n + h)
            gh = g[:, head(h)]
            att = attended[half * chunks + h // each][:, head(h % each)].astype(F32)
            state = carried[half * chunks + h // each][head(h % each), :]
            normed[:, at] = (gain[:, at] * att * inv).astype(BF16)
            gs = dot(gh, v[:, head(h)], NT)
            gs = jnp.where(seen, gs, 0.0).astype(BF16)
            whole = dot(gs, k[:, head(h)], NN) + keep * dot(gh, state, NT)
            grad_q[:, at] = whole.astype(BF16)
            part_k[:, at] = dot(gs, q[:, at], TN)
            part_v[:, at] = dot(scores[half * n + h], gh, TN)
        span = slice(half * width, (half + 1) * width)
        for i, (held, out) in enumerate(((normed, normed_hbm), (grad_q, grad_q_hbm))):
            copies.append(
                pltpu.make_async_copy(
                    held.at[:, span], out.at[:, columns(half, width)], sems.at[2 * half + i]
                )
            )
            copies[-1].start()
    for copy in copies:
        copy.wait()


def last_kernel(parts, chunks, row, part_k, part_v, *rest):
    n = len(parts)
    k_hbm, v_hbm, grad_k, grad_v, sems = rest[-5:]
    rows, width = part_k.shape
    keep = in_doc(row, rows - 1)
    last = tag(row, rows - 1)
    copies = []
    for i, (half, chunk) in enumerate(parts):
        states, k, v = rest[3 * i:3 * i + 3]
        size = states.shape[0] - TAG
        same = states[size:size + 1, :] == last
        at_core = core() if half == 0 else 1 - core()
        for h in range(size // HD):
            own = head(chunk * (size // HD) + h)
            at = head((half * chunks + chunk) * (size // HD) + h)
            mine = len(copies) // 2
            later = jnp.where(same, states[head(h), :], 0.0).astype(BF16)
            new_k = part_k[:, at] + keep * dot(v[:, own], later, NT)
            new_v = part_v[:, at] + keep * dot(k[:, own], later, NN)
            grad_k[:, head(mine)] = new_k.astype(BF16)
            grad_v[:, head(mine)] = new_v.astype(BF16)
            start = at_core * (width // 2) + chunk * size + h * HD
            span = pl.ds(pl.multiple_of(start, HD), HD)
            for j, (held, out) in enumerate(((grad_k, k_hbm), (grad_v, v_hbm))):
                copies.append(
                    pltpu.make_async_copy(
                        held.at[:, head(mine)], out.at[:, span], sems.at[2 * mine + j]
                    )
                )
                copies[-1].start()
    for copy in copies:
        copy.wait()


def call(kernel, fixed, outs, args, after=(), scratch=(), aliases={}):
    spaces = [HBM if isinstance(x, list) else VMEM for x in args] + [ANY] * len(after)
    args = [
        pltpu.with_memory_space_constraint(x[0], HBM) if isinstance(x, list) else x for x in args
    ]
    return pl.pallas_call(
        lambda *refs: kernel(*fixed, *refs),
        out_shape=[jax.ShapeDtypeStruct(*out[:2]) for out in outs],
        in_specs=[pl.BlockSpec(memory_space=space) for space in spaces],
        out_specs=[pl.BlockSpec(memory_space=(*out, VMEM)[2]) for out in outs],
        scratch_shapes=scratch,
        input_output_aliases=aliases,
        compiler_params=pltpu.CompilerParams(vmem_limit_bytes=40 * 1024 * 1024),
        name=kernel.__name__[:-7],
    )(*args, *after)


def carry(mine, other, chunks, backward, beside, finish):
    blocks = lax.axis_size("ctx")
    step = -2 if backward else 2

    def swap(value):
        return lax.ppermute(value, "ctx", [(i, i ^ 1) for i in range(blocks)])

    def hop(value):
        return lax.ppermute(value, "ctx", [(i, (i + step) % blocks) for i in range(blocks)])

    sent = other()
    came = swap(sent)
    mine = mine(sent)
    size = (mine.shape[0] - TAG) // chunks
    chunk = ((size + TAG, HD), F32)
    both = call(pair_kernel, [backward], [chunk] * chunks, [mine, came])
    once = [hop(b) for b in both]
    work, token = beside(both[-1])
    window = [call(merge_kernel, [], [chunk], [b, o], [token])[0] for b, o in zip(both, once)]
    entering = [hop(w) for w in window]
    ready = []
    for i, e in enumerate(entering):
        kept, send = call(split_kernel, [backward, i], [chunk] * 2, [e, mine, came])
        ready += [((0, i), kept), ((1, i), swap(send))]
    finish(*map(list, zip(*ready[:-1])), work)
    finish(*map(list, zip(*ready[-1:])), work)
    return work


CHUNKS = 2


def local(queries, key_rows, value_rows, grad_out, doc_ids, out_gain):
    rows, width = queries.shape
    heads = width // HD
    part_width = width // 2
    ranks = lax.axis_size("head")
    ids = doc_ids.reshape(1, rows)
    gain = out_gain.reshape(1, width)
    wide, half, sums = ((rows, width), F32), ((rows, part_width), BF16), ((TAG, rows), F32)
    state = ((part_width + TAG, HD), F32)

    held = {}

    def make_state(which, after=()):
        out, held["k", which], held["v", which], *row = call(
            state_kernel, [which], [state, half, half] + [((1, rows), jnp.int32)] * which,
            [[ids] if which else held["row"], [key_rows], [value_rows]],
            after=after, scratch=[DMA((3,))],
        )
        if which:
            (held["row"],) = row
        return out

    def local_work(token):
        out = call(
            local_kernel, [],
            [((heads, rows, rows), BF16), wide, ((rows, width), BF16), wide, ((1, width), F32)],
            [held["row"], *k, *v, [queries], [grad_out], [gain]],
            after=[token], scratch=[VMEM((rows, width), BF16), DMA((6,))],
        )
        return out, out[1]

    k, v = [], []

    def own_state(sent):
        out = make_state(0, [sent])
        k.extend(held["k", i] for i in range(2))
        v.extend(held["v", i] for i in range(2))
        return out

    attended, carried, stats = {}, {}, []
    piece = part_width // CHUNKS

    def attend(parts, states, work):
        _, part, q, weighted, _ = work
        n = len(parts)
        out = call(
            attend_kernel, [parts, CHUNKS],
            [((rows, piece), BF16)] * n + [((piece, HD), BF16)] * n + [sums],
            [held["row"], q, part, weighted, *states, *stats[-1:]],
        )
        attended.update(zip(parts, out))
        carried.update(zip(parts, out[n:]))
        stats.append(out[-1])

    work = carry(own_state, lambda: make_state(1), CHUNKS, False, local_work, attend)
    scores, part, q, weighted, gain = work
    order = [(which, i) for which in range(2) for i in range(CHUNKS)]
    stats = stats[-1:]
    stats += [
        lax.ppermute(stats[0], "head", [(i, i ^ apart) for i in range(ranks)])
        for apart in range(1, ranks)
    ]

    def make_grad(which, after=()):
        held["g", which], out = call(
            grad_kernel, [which, CHUNKS, ranks], [half, state],
            [held["row"], q, weighted, *(attended[which, i] for i in range(CHUNKS)), *stats],
            after=after,
        )
        return out

    def back_work(token):
        out = call(
            back_kernel, [CHUNKS, ranks], [((rows, width), BF16, HBM)] * 2 + [wide, wide],
            [held["row"], q, scores, gain, *k, *v, held["g", 0], held["g", 1],
             *(attended[x] for x in order), *(carried[x] for x in order), *stats],
            after=[token],
            scratch=[VMEM((rows, width), BF16), VMEM((rows, width), BF16), DMA((4,))],
        )
        return out, out[2]

    done = []

    def last(parts, states, work):
        args = [held["row"], work[2], work[3]]
        for (which, _), state in zip(parts, states):
            args += [state, k[which], v[which]]
        n = len(args)
        size = len(parts) * piece
        out = call(
            last_kernel, [parts, CHUNKS], [((rows, width), BF16, HBM)] * 2, args,
            after=done[-1] if done else (),
            scratch=[VMEM((rows, size), BF16), VMEM((rows, size), BF16), DMA((2 * size // HD,))],
            aliases={n: 0, n + 1: 1} if done else {},
        )
        done.append(out)

    work = carry(
        lambda sent: make_grad(0, [sent]), lambda: make_grad(1), CHUNKS, True, back_work, last
    )
    return work[0], work[1], *done[-1]


def solution(mesh):
    cut = P("ctx", "head")
    return jax.shard_map(
        local,
        mesh=mesh,
        in_specs=(cut, cut, cut, cut, P("ctx"), P("head")),
        out_specs=(cut, cut, cut, cut),
        check_vma=False,
    )
```

```python
import jax
import jax.numpy as jnp
from jax import lax
from jax.experimental import pallas as pl
from jax.experimental.pallas import tpu as pltpu
from jax.sharding import PartitionSpec as P

HEADS = 32
HD = 128
TAG = 8
F32 = jnp.float32
BF16 = jnp.bfloat16
VMEM, HBM, ANY = pltpu.VMEM, pltpu.HBM, pl.ANY
DMA = pltpu.SemaphoreType.DMA
NN = ((1,), (0,))
NT = ((1,), (1,))
TN = ((0,), (0,))


def dot(a, b, dims):
    return lax.dot_general(a, b, (dims, ((), ())), preferred_element_type=F32)


def head(h):
    return slice(h * HD, (h + 1) * HD)


def core():
    return lax.rem(lax.axis_index("ctx"), 2)


def columns(half, width):
    at = core() if half == 0 else 1 - core()
    return pl.ds(pl.multiple_of(at * width, width), width)


def as_column(row):
    return jnp.transpose(jnp.broadcast_to(row, (HD, row.shape[1])))


def in_doc(row_ref, at):
    row = row_ref[...].astype(F32)
    which = jnp.broadcast_to(row[:, at:at + 1], (row.shape[1], HD))
    return (as_column(row) == which).astype(F32)


def tag(row_ref, at):
    return jnp.broadcast_to(row_ref[:, at:at + 1].astype(F32), (1, HD))


def visible(row_ref):
    rows = row_ref.shape[1]
    row = row_ref[...].astype(F32)
    column = as_column(row)
    column = jnp.concatenate([column] * (rows // HD), axis=1)
    t = lax.broadcasted_iota(jnp.int32, (rows, rows), 0)
    s = lax.broadcasted_iota(jnp.int32, (rows, rows), 1)
    return (column == jnp.broadcast_to(row, (rows, rows))) & (t >= s)


def state_kernel(half, row, k_hbm, v_hbm, *rest):
    if half:
        out, k, v, row_out, sems = rest[-5:]
    else:
        out, k, v, sems = rest[-4:]
    rows, width = k.shape
    span = columns(half, width)
    copies = [
        pltpu.make_async_copy(k_hbm.at[:, span], k, sems.at[1]),
        pltpu.make_async_copy(v_hbm.at[:, span], v, sems.at[2]),
    ]
    if half:
        copies.insert(0, pltpu.make_async_copy(row, row_out, sems.at[0]))
        row = row_out
    for copy in copies:
        copy.start()
    if half:
        copies.pop(0).wait()
    keep = in_doc(row, rows - 1).astype(BF16)
    out[width:, :] = jnp.broadcast_to(tag(row, rows - 1), (TAG, HD))
    for copy in copies:
        copy.wait()
    for h in range(width // HD):
        out[head(h), :] = dot(k[:, head(h)] * keep, v[:, head(h)], TN)


def add_into(out, near, far, near_lo, far_lo):
    size = out.shape[0] - TAG
    near_tag = near[near.shape[0] - TAG:, :]
    same = near_tag[0:1, :] == far[far.shape[0] - TAG:far.shape[0] - TAG + 1, :]
    here = far[far_lo:far_lo + size, :]
    out[:size, :] = near[near_lo:near_lo + size, :] + jnp.where(same, here, 0.0)
    out[size:, :] = near_tag


def pair_kernel(backward, mine, came, *outs):
    size = outs[0].shape[0] - TAG
    upstream = core() == int(backward)

    def fill(down, up):
        for i, out in enumerate(outs):
            add_into(out, down, up, i * size, i * size)

    pl.when(upstream)(lambda: fill(came, mine))
    pl.when(jnp.logical_not(upstream))(lambda: fill(mine, came))


def merge_kernel(near, far, *rest):
    add_into(rest[-1], near, far, 0, 0)


def split_kernel(backward, part, entering, mine, came, *rest):
    keep, send = rest[-2:]
    size = entering.shape[0] - TAG
    upstream = core() == int(backward)

    def fill(to_up, to_down, up):
        to_up[...] = entering[...]
        add_into(to_down, up, entering, part * size, 0)

    pl.when(upstream)(lambda: fill(keep, send, mine))
    pl.when(jnp.logical_not(upstream))(lambda: fill(send, keep, came))


def local_kernel(row, k0, k1, v0, v1, q_hbm, grad_hbm, gain_hbm, *rest):
    scores, part, q, weighted, gain, grad, sems = rest[-7:]
    rows, width = k0.shape
    copies = []
    for i, (hbm, held) in enumerate(((q_hbm, q), (gain_hbm, gain), (grad_hbm, grad))):
        for half in range(2):
            at = slice(half * width, (half + 1) * width)
            copies.append(
                pltpu.make_async_copy(
                    hbm.at[:, columns(half, width)], held.at[:, at], sems.at[2 * i + half]
                )
            )
            copies[-1].start()
    seen = visible(row)
    copies[0].wait()
    copies[1].wait()
    n = width // HD
    for h in range(2 * n):
        k, v = (k0, v0) if h < n else (k1, v1)
        sc = dot(q[:, head(h)], k[:, head(h % n)], NT)
        sc = jnp.where(seen, sc, 0.0).astype(BF16)
        scores[h] = sc
        part[:, head(h)] = dot(sc, v[:, head(h % n)], NN)
    for copy in copies[2:]:
        copy.wait()
    for h in range(2 * n):
        weighted[:, head(h)] = gain[:, head(h)] * grad[:, head(h)].astype(F32)


def attend_kernel(parts, chunks, row, q, part, weighted, *rest):
    n = len(parts)
    came, sofar = rest[:n], rest[n:n + 1]
    outs, stats = rest[-2 * n - 1:-1], rest[-1]
    rows, width = q.shape
    keep = in_doc(row, 0)
    first = tag(row, 0)
    square = jnp.zeros((rows, HD), F32)
    inner = jnp.zeros((rows, HD), F32)
    for i, (half, chunk) in enumerate(parts):
        states, attended, carried = came[i], outs[i], outs[n + i]
        size = states.shape[0] - TAG
        same = states[size:size + 1, :] == first
        for h in range(size // HD):
            at = head((half * chunks + chunk) * (size // HD) + h)
            state = jnp.where(same, states[head(h), :], 0.0).astype(BF16)
            carried[head(h), :] = state
            att = (part[:, at] + keep * dot(q[:, at], state, NN)).astype(BF16)
            attended[:, head(h)] = att
            att = att.astype(F32)
            square = square + att * att
            inner = inner + weighted[:, at] * att
    ones = jnp.ones((TAG, HD), F32)
    upper = lax.broadcasted_iota(jnp.int32, (TAG, rows), 0) < TAG // 2
    exact = lax.Precision.HIGHEST
    sums = [
        lax.dot_general(ones, x, (NT, ((), ())), precision=exact, preferred_element_type=F32)
        for x in (square, inner)
    ]
    sums = jnp.where(upper, sums[0], sums[1])
    stats[...] = sums + sofar[0][...] if len(rest) > 3 * n + 1 else sums


def norm_scales(parts):
    feats = HEADS * HD
    total = parts[0][...]
    for x in parts[1:]:
        total = total + x[...]
    inv = lax.rsqrt(total[0:1, :] / feats + 1e-06)
    back = inv * inv * inv * (total[TAG - 1:TAG, :] / feats)
    return as_column(inv), as_column(back)


def grad_kernel(half, chunks, ranks, row, q, weighted, *rest):
    *_, g_out, out = rest if half else rest[:-1]
    rows, width = g_out.shape
    each = width // HD // chunks
    keep = in_doc(row, 0).astype(BF16)
    inv, back = norm_scales(rest[chunks:chunks + ranks])
    for h in range(width // HD):
        at = head(half * (width // HD) + h)
        att = rest[h // each][:, head(h % each)].astype(F32)
        g = (inv * weighted[:, at] - att * back).astype(BF16)
        g_out[:, head(h)] = g
        out[head(h), :] = dot(q[:, at] * keep, g, TN)
    out[width:, :] = jnp.broadcast_to(tag(row, 0), (TAG, HD))
    if not half:
        normed = rest[-1]
        pieces = (*rest[:chunks], *rest[chunks + ranks:2 * chunks + ranks])
        gain = rest[2 * chunks + ranks]
        for h in range(2 * width // HD):
            att = pieces[h // each][:, head(h % each)].astype(F32)
            normed[:, head(h)] = (gain[:, head(h)] * att * inv).astype(BF16)


def back_kernel(chunks, row, q, scores, normed, k0, k1, v0, v1, g0, g1, *rest):
    carried = rest[:2 * chunks]
    normed_hbm, grad_q_hbm, part_k, part_v, grad_q, sems = rest[-6:]
    rows, width = k0.shape
    keep = in_doc(row, 0)
    seen = visible(row)
    n = width // HD
    copies = []

    def send(half, i, held, out):
        span = slice(half * width, (half + 1) * width)
        copies.append(
            pltpu.make_async_copy(
                held.at[:, span], out.at[:, columns(half, width)], sems.at[2 * half + i]
            )
        )
        copies[-1].start()

    send(0, 0, normed, normed_hbm)
    send(1, 0, normed, normed_hbm)
    each = n // chunks
    for half, (k, v, g) in enumerate(((k0, v0, g0), (k1, v1, g1))):
        for h in range(n):
            at = head(half * n + h)
            gh = g[:, head(h)]
            state = carried[half * chunks + h // each][head(h % each), :]
            gs = dot(gh, v[:, head(h)], NT)
            gs = jnp.where(seen, gs, 0.0).astype(BF16)
            whole = dot(gs, k[:, head(h)], NN) + keep * dot(gh, state, NT)
            grad_q[:, at] = whole.astype(BF16)
            part_k[:, at] = dot(gs, q[:, at], TN)
            part_v[:, at] = dot(scores[half * n + h], gh, TN)
        send(half, 1, grad_q, grad_q_hbm)
    for copy in copies:
        copy.wait()


def last_kernel(parts, chunks, row, part_k, part_v, *rest):
    n = len(parts)
    k_hbm, v_hbm, grad_k, grad_v, sems = rest[-5:]
    rows, width = part_k.shape
    keep = in_doc(row, rows - 1)
    last = tag(row, rows - 1)
    copies = []
    for i, (half, chunk) in enumerate(parts):
        states, k, v = rest[3 * i:3 * i + 3]
        size = states.shape[0] - TAG
        same = states[size:size + 1, :] == last
        at_core = core() if half == 0 else 1 - core()
        for h in range(size // HD):
            own = head(chunk * (size // HD) + h)
            at = head((half * chunks + chunk) * (size // HD) + h)
            mine = len(copies) // 2
            later = jnp.where(same, states[head(h), :], 0.0).astype(BF16)
            new_k = part_k[:, at] + keep * dot(v[:, own], later, NT)
            new_v = part_v[:, at] + keep * dot(k[:, own], later, NN)
            grad_k[:, head(mine)] = new_k.astype(BF16)
            grad_v[:, head(mine)] = new_v.astype(BF16)
            start = at_core * (width // 2) + chunk * size + h * HD
            span = pl.ds(pl.multiple_of(start, HD), HD)
            for j, (held, out) in enumerate(((grad_k, k_hbm), (grad_v, v_hbm))):
                copies.append(
                    pltpu.make_async_copy(
                        held.at[:, head(mine)], out.at[:, span], sems.at[2 * mine + j]
                    )
                )
                copies[-1].start()
    for copy in copies:
        copy.wait()


def call(kernel, fixed, outs, args, after=(), scratch=(), aliases={}):
    spaces = [HBM if isinstance(x, list) else VMEM for x in args] + [ANY] * len(after)
    args = [
        pltpu.with_memory_space_constraint(x[0], HBM) if isinstance(x, list) else x for x in args
    ]
    return pl.pallas_call(
        lambda *refs: kernel(*fixed, *refs),
        out_shape=[jax.ShapeDtypeStruct(*out[:2]) for out in outs],
        in_specs=[pl.BlockSpec(memory_space=space) for space in spaces],
        out_specs=[pl.BlockSpec(memory_space=(*out, VMEM)[2]) for out in outs],
        scratch_shapes=scratch,
        input_output_aliases=aliases,
        compiler_params=pltpu.CompilerParams(vmem_limit_bytes=40 * 1024 * 1024),
        name=kernel.__name__[:-7],
    )(*args, *after)


def carry(mine, other, chunks, backward, beside, finish):
    blocks = lax.axis_size("ctx")
    step = -2 if backward else 2

    def swap(value):
        return lax.ppermute(value, "ctx", [(i, i ^ 1) for i in range(blocks)])

    def hop(value):
        return lax.ppermute(value, "ctx", [(i, (i + step) % blocks) for i in range(blocks)])

    sent = other()
    came = swap(sent)
    mine = mine(sent)
    size = (mine.shape[0] - TAG) // chunks
    chunk = ((size + TAG, HD), F32)
    both = call(pair_kernel, [backward], [chunk] * chunks, [mine, came])
    once = [hop(b) for b in both]
    work, token = beside(both[-1])
    window = [call(merge_kernel, [], [chunk], [b, o], [token])[0] for b, o in zip(both, once)]
    entering = [hop(w) for w in window]
    ready = []
    for i, e in enumerate(entering):
        kept, send = call(split_kernel, [backward, i], [chunk] * 2, [e, mine, came])
        ready += [((0, i), kept), ((1, i), swap(send))]
    finish(*map(list, zip(*ready[:-1])), work)
    finish(*map(list, zip(*ready[-1:])), work)
    return work


CHUNKS = 2


def local(queries, key_rows, value_rows, grad_out, doc_ids, out_gain):
    rows, width = queries.shape
    heads = width // HD
    part_width = width // 2
    ranks = lax.axis_size("head")
    ids = doc_ids.reshape(1, rows)
    gain = out_gain.reshape(1, width)
    wide, half, sums = ((rows, width), F32), ((rows, part_width), BF16), ((TAG, rows), F32)
    state = ((part_width + TAG, HD), F32)

    held = {}

    def make_state(which, after=()):
        out, held["k", which], held["v", which], *row = call(
            state_kernel, [which], [state, half, half] + [((1, rows), jnp.int32)] * which,
            [[ids] if which else held["row"], [key_rows], [value_rows]],
            after=after, scratch=[DMA((3,))],
        )
        if which:
            (held["row"],) = row
        return out

    def local_work(token):
        out = call(
            local_kernel, [],
            [((heads, rows, rows), BF16), wide, ((rows, width), BF16), wide, ((1, width), F32)],
            [held["row"], *k, *v, [queries], [grad_out], [gain]],
            after=[token], scratch=[VMEM((rows, width), BF16), DMA((6,))],
        )
        return out, out[1]

    k, v = [], []

    def own_state(sent):
        out = make_state(0, [sent])
        k.extend(held["k", i] for i in range(2))
        v.extend(held["v", i] for i in range(2))
        return out

    attended, carried, stats = {}, {}, []
    piece = part_width // CHUNKS

    def attend(parts, states, work):
        _, part, q, weighted, _ = work
        n = len(parts)
        out = call(
            attend_kernel, [parts, CHUNKS],
            [((rows, piece), BF16)] * n + [((piece, HD), BF16)] * n + [sums],
            [held["row"], q, part, weighted, *states, *stats[-1:]],
        )
        attended.update(zip(parts, out))
        carried.update(zip(parts, out[n:]))
        stats.append(out[-1])

    work = carry(own_state, lambda: make_state(1), CHUNKS, False, local_work, attend)
    scores, part, q, weighted, gain = work
    order = [(which, i) for which in range(2) for i in range(CHUNKS)]
    stats = stats[-1:]
    stats += [
        lax.ppermute(stats[0], "head", [(i, (i + apart) % ranks) for i in range(ranks)])
        for apart in range(1, ranks)
    ]

    def make_grad(which, after=()):
        pieces = [[attended[w, i] for i in range(CHUNKS)] for w in range(2)]
        extra = [] if which else [*pieces[1], gain]
        held["g", which], out, *normed = call(
            grad_kernel, [which, CHUNKS, ranks],
            [half, state] + [((rows, width), BF16)] * (1 - which),
            [held["row"], q, weighted, *pieces[which], *stats, *extra], after=after,
        )
        if not which:
            (held["normed"],) = normed
        return out

    def back_work(token):
        out = call(
            back_kernel, [CHUNKS], [((rows, width), BF16, HBM)] * 2 + [wide, wide],
            [held["row"], q, scores, held["normed"], *k, *v, held["g", 0], held["g", 1],
             *(carried[x] for x in order)],
            after=[token],
            scratch=[VMEM((rows, width), BF16), DMA((4,))],
        )
        return out, out[2]

    done = []

    def last(parts, states, work):
        args = [held["row"], work[2], work[3]]
        for (which, _), state in zip(parts, states):
            args += [state, k[which], v[which]]
        n = len(args)
        size = len(parts) * piece
        out = call(
            last_kernel, [parts, CHUNKS], [((rows, width), BF16, HBM)] * 2, args,
            after=done[-1] if done else (),
            scratch=[VMEM((rows, size), BF16), VMEM((rows, size), BF16), DMA((2 * size // HD,))],
            aliases={n: 0, n + 1: 1} if done else {},
        )
        done.append(out)

    work = carry(
        lambda sent: make_grad(0, [sent]), lambda: make_grad(1), CHUNKS, True, back_work, last
    )
    return work[0], work[1], *done[-1]


def solution(mesh):
    cut = P("ctx", "head")
    return jax.shard_map(
        local,
        mesh=mesh,
        in_specs=(cut, cut, cut, cut, P("ctx"), P("head")),
        out_specs=(cut, cut, cut, cut),
        check_vma=False,
    )
```
